32 devices in a mesh: role: 2 (over y), dev: 16 (over z, x, core).
Axes of the slice: x: 2, y: 2, z: 4, core: 2. Of those that a mesh axis runs over, the one named last changes fastest.
Arguments:
- tokens: bfloat16 [16384, 1024], P(('role', 'dev')), may hold values from -6 to 6
- expert_ids: int32 [16384, 1], P(('role', 'dev')), may hold values from 0 to 31; in each aligned block of 512 rows (0 to 511, 512 to 1023, ...) at most 32 rows name the same one
- w_qkv: bfloat16 [1024, 3072], P(('role', 'dev')), may hold values from -2 to 2
- w_attn_out: bfloat16 [1024, 1024], P(('role', 'dev')), may hold values from -0.1875 to 0.1875
- gain_attn: bfloat16 [1024], replicated, may hold values from 0.5 to 1.5
- gain_expert: bfloat16 [1024], replicated, may hold values from 0.5 to 1.5
- router: bfloat16 [1024, 32], replicated, may hold values from -0.375 to 0.375
- expert_in: bfloat16 [32, 1024, 2816], P(('role', 'dev')), may hold values from -0.1875 to 0.1875
- expert_out: bfloat16 [32, 2816, 1024], P(('role', 'dev')), may hold values from -0.109375 to 0.109375
- capacity: int32 [32], replicated, may hold values from 256 to 1023
- swap_list: int32 [8], replicated, may hold values from 0 to 15, as said below
Outputs:
- mixed: bfloat16 [16384, 1024], P(('role', 'dev'))
The draws below stay inside these ranges and needn't reach their ends.
Inputs may be any that keep to these rules, and one draw needn't show every extreme that they name: `expert_ids`: in the rows of one device no expert is named more than 32 times, a bound that some block reaches. `swap_list`: entries are distinct.
All inputs are finite; a program needn't handle non-finite values.
Results may differ from the reference program's by a relative error of at most 0.0052.
Values may be sent and summed in bfloat16 or wider, within the bound.
No kernel may reach another device: no remote copies, remote signals or barrier semaphores. Data moves between devices by JAX's collectives and lax.ppermute only.
A program may use at most 128 MiB of HBM per device.

```python
import math
import jax
import jax.numpy as jnp
import numpy as np
from jax import lax

D = 1024
HEADS = 16
FF = 2816
TOK_DEV = 512
EXPERTS = 32
C = 32
PAIRS = 8
TOKENS = 16384
N_ROLE = 2
N_DEV = 16


def draw_tokens(key, part):
    keys = jax.random.split(key, 1)
    base = jax.random.normal(keys[0], (TOKENS, D), jnp.float32)
    return jnp.clip(base, -6.0, 6.0).astype(jnp.bfloat16)


def draw_w_qkv(key, part):
    keys = jax.random.split(key, 1)
    base = jax.random.normal(keys[0], (D, 3 * D), jnp.float32) * D ** (-0.5)
    return jnp.clip(base, -2.0, 2.0).astype(jnp.bfloat16)


def draw_swap_list(key, part):
    return jax.random.permutation(key, N_DEV)[:PAIRS].astype(jnp.int32)


def set_ends(array, rng, least, high):
    index_at = [jax.random.randint(jax.random.fold_in(rng, axis), (), 0, length) for axis, length in enumerate(array.shape)]
    main_axis = array.shape.index(max(array.shape))
    next_to = index_at[:main_axis] + [(index_at[main_axis] + 1) % array.shape[main_axis]] + index_at[main_axis + 1:]
    return array.at[tuple(index_at)].set(least).at[tuple(next_to)].set(high)


def levels(stream_key, shape, pieces, smallest, largest):
    level, own = 1.0, jax.random.fold_in(stream_key, 6)
    for dim, blocks in pieces:
        heights = jnp.exp(jax.random.uniform(jax.random.fold_in(own, dim), (blocks,), jnp.float32, smallest / len(pieces), largest / len(pieces)))
        level = level * jnp.repeat(heights, shape[dim] // blocks).reshape([-1 if axis == dim else 1 for axis in range(len(shape))])
    return level


def deal_out(stream_key, own, number, rows, count, top, reach, slope):
    sequence = jax.random.permutation(stream_key, count)
    heavy_load, ordinary = load_shares(count, rows * top, reach, slope, True), load_shares(count, rows * top, reach, slope, False)
    places = jnp.arange(count)

    def named(tallies, rotation):
        used = int((tallies > 0).sum())
        fixed = max(1, used // 4)
        shifted = fixed + (places - fixed + rotation * (used - fixed)) % max(1, count - fixed)
        return jnp.zeros((count,), jnp.int32).at[sequence[jnp.where(places < fixed, places, shifted)]].set(jnp.asarray(tallies, jnp.int32))

    tallies = jnp.where(number % 4 == 0, named(heavy_load, number // 4), named(ordinary, number - number // 4 - 1))
    mixed = jax.random.permutation(jax.random.fold_in(own, 3), count)
    source_of, taker = mixed[0:count // 2 * 2:2], mixed[1:count // 2 * 2:2]
    margin = jnp.minimum(tallies[source_of] - 1, reach - tallies[taker]) // 2
    margin = jnp.where((source_of == sequence[0]) | (taker == sequence[0]) | (tallies[taker] == 0), 0, jnp.maximum(margin, 0))
    shifted = jax.random.randint(jax.random.fold_in(own, 4), (count // 2,), 0, 1 << 20) % (margin + 1)
    tallies = tallies.at[source_of].add(-shifted).at[taker].add(shifted)
    labels = jnp.searchsorted(jnp.cumsum(tallies), jnp.arange(rows * top), side="right").astype(jnp.int32)
    listing = labels.reshape(top, rows).T
    listing = listing[jax.random.permutation(jax.random.fold_in(own, 1), rows)]
    rotation = jax.random.randint(jax.random.fold_in(own, 2), (rows, 1), 0, top)
    return jnp.take_along_axis(listing, (jnp.arange(top)[None, :] + rotation) % top, axis=1)


def load_shares(count, total, most, slope, full):
    weights = [(1 << 20) // math.isqrt(grade ** slope) + 1 for grade in range(1, count + 1)]
    largest = most if full else min(most, max(-(-total // count), total * weights[0] // sum(weights)))
    least = 1 if total - largest >= count - 1 else 0
    holding, rest = [largest] + [least] * (count - 1), total - largest - least * (count - 1)
    while rest > 0:
        movable = [i for i in range(1, count) if holding[i] < largest] or [i for i in range(1, count) if holding[i] < most]
        pool, remaining = sum([weights[i] for i in movable]), rest
        for i in movable:
            more = min(most - holding[i], max(1, remaining * weights[i] // pool), rest)
            holding[i] = holding[i] + more
            rest = rest - more
    return np.array(holding)


def centred(rng, dims, scale, most, cuts=(), kind=jnp.bfloat16):
    gain = levels(rng, dims, cuts, -0.22, 0.18) if cuts else 1.0
    drawn = jax.random.normal(rng, dims, jnp.float32) * scale * gain
    return jnp.minimum(jnp.maximum(drawn, -most), most).astype(kind)


def setup_inputs(seed: int = 0) -> dict:
    streams_of = jax.random.split(jax.random.key(seed), 12)
    tokens = draw_tokens(jax.random.fold_in(streams_of[11], 71), 0)
    expert_ids_keys = jax.random.split(jax.random.fold_in(streams_of[1], 1), TOKENS // TOK_DEV)
    expert_ids_turns = jax.random.permutation(jax.random.fold_in(streams_of[1], 3), TOKENS // TOK_DEV)
    expert_ids = jax.vmap(lambda own, number: deal_out(jax.random.fold_in(streams_of[1], 2), own, number, TOK_DEV, EXPERTS, 1, C, 2))(expert_ids_keys, expert_ids_turns).reshape((TOKENS, 1))
    w_qkv = draw_w_qkv(jax.random.fold_in(streams_of[11], 71), 0)
    w_attn_out = centred(streams_of[3], (D, D), D ** -0.5, 0.1875, ((0, 32),))
    gain_attn = jnp.clip(1.0 + 0.1 * jax.random.normal(streams_of[4], (D,), jnp.float32), 0.5, 1.5).astype(jnp.bfloat16)
    gain_expert = jnp.clip(1.0 + 0.1 * jax.random.normal(streams_of[5], (D,), jnp.float32), 0.5, 1.5).astype(jnp.bfloat16)
    router = centred(streams_of[6], (D, EXPERTS), (D // 4) ** -0.5, 0.375)
    expert_in = centred(streams_of[7], (EXPERTS, D, FF), D ** -0.5, 0.1875, ((0, 32),))
    expert_out = centred(streams_of[8], (EXPERTS, FF, D), FF ** -0.5, 0.109375, ((0, 32),))
    capacity = set_ends(jax.random.randint(streams_of[9], (EXPERTS,), TOK_DEV // 2, 2 * TOK_DEV), jax.random.fold_in(streams_of[9], 1), TOK_DEV // 2, (2 * TOK_DEV) - 1).astype(jnp.int32)
    swap_list = draw_swap_list(jax.random.fold_in(streams_of[11], 71), 0)
    return dict(tokens=tokens, expert_ids=expert_ids, w_qkv=w_qkv, w_attn_out=w_attn_out, gain_attn=gain_attn, gain_expert=gain_expert, router=router, expert_in=expert_in, expert_out=expert_out, capacity=capacity, swap_list=swap_list)


def rms_scale(values, gain_vector):
    mean_sq = lax.optimization_barrier(jnp.mean(values * values, axis=-1, keepdims=True))
    return values * lax.rsqrt(mean_sq + 1e-06) * gain_vector.astype(jnp.float32)

def self_attend(qkv_rows, head_count):
    row_count = qkv_rows.shape[0]
    model_width = qkv_rows.shape[1] // 3
    head_size = model_width // head_count
    queries = qkv_rows[:, :model_width].reshape(row_count, head_count, head_size).astype(jnp.float32)
    keys_all = qkv_rows[:, model_width:2 * model_width].reshape(row_count, head_count, head_size).astype(jnp.float32)
    values = qkv_rows[:, 2 * model_width:].reshape(row_count, head_count, head_size).astype(jnp.float32)
    scores = jnp.einsum('shd,thd->hst', queries, keys_all) * head_size ** (-0.5)
    row_max = lax.optimization_barrier(jnp.max(scores, axis=-1, keepdims=True))
    weights = jnp.exp(scores - row_max)
    soft_weights = (weights / lax.optimization_barrier(jnp.sum(weights, axis=-1, keepdims=True))).astype(jnp.bfloat16)
    context = jnp.einsum('hst,thd->shd', soft_weights.astype(jnp.float32), values)
    return context.reshape(row_count, model_width).astype(jnp.bfloat16)

def reference(tokens, expert_ids, w_qkv, w_attn_out, gain_attn, gain_expert, router, expert_in, expert_out, capacity, swap_list):
    device_count = N_ROLE * N_DEV
    sequences = tokens.reshape(device_count, TOK_DEV, D)

    def one_sequence(block):
        residual = block.astype(jnp.float32)
        normed = rms_scale(residual, gain_attn).astype(jnp.bfloat16)
        qkv_rows = jnp.dot(normed, w_qkv, preferred_element_type=jnp.float32).astype(jnp.bfloat16)
        context = self_attend(qkv_rows, HEADS)
        attended = jnp.dot(context, w_attn_out, preferred_element_type=jnp.float32)
        return residual + attended
    hidden = lax.map(one_sequence, sequences).reshape(device_count * TOK_DEV, D)
    normed_ffn = rms_scale(hidden, gain_expert).astype(jnp.bfloat16)
    logits = jnp.dot(normed_ffn, router, preferred_element_type=jnp.float32)
    chosen = expert_ids[:, 0].astype(jnp.int32)
    gate = jax.nn.sigmoid(jnp.take_along_axis(logits, chosen[:, None], axis=1)[:, 0])
    expert_range = jnp.arange(EXPERTS, dtype=jnp.int32)
    one_hot = (chosen[:, None] == expert_range[None, :]).astype(jnp.int32)
    earlier = jnp.cumsum(one_hot, axis=0) - one_hot
    position = jnp.take_along_axis(earlier, chosen[:, None], axis=1)[:, 0].astype(jnp.int32)
    flagged = jnp.any(swap_list[:, None] == jnp.arange(N_DEV, dtype=jnp.int32)[None, :], axis=0)
    dev_index = expert_range % N_DEV
    role_index = expert_range // N_DEV
    location = jnp.where(flagged[dev_index], (1 - role_index) * N_DEV + dev_index, expert_range).astype(jnp.int32)
    limit = capacity[location][chosen]
    kept = position < limit
    slot_count = EXPERTS * C
    buffer = jnp.zeros((EXPERTS, slot_count, D), jnp.bfloat16).at[chosen, position].set(normed_ffn)

    def one_expert(operands):
        rows_in, weight_in, weight_out = operands
        activ = jnp.maximum(jnp.dot(rows_in, weight_in, preferred_element_type=jnp.float32), 0.0).astype(jnp.bfloat16)
        return jnp.dot(activ, weight_out, preferred_element_type=jnp.float32).astype(jnp.bfloat16)
    results = lax.map(one_expert, (buffer, expert_in, expert_out))
    picked = results[chosen, position].astype(jnp.float32)
    mixed = hidden + jnp.where(kept, gate, jnp.zeros_like(gate))[:, None] * picked
    return mixed.astype(jnp.bfloat16)
```

```python
import jax
import jax.numpy as jnp
from jax import lax
from jax.sharding import PartitionSpec as P

HEADS = 16
AXES = ("role", "dev")
LANES = 128


def rms_scale(values, gain_vector):
    mean_sq = jnp.mean(values * values, axis=-1, keepdims=True)
    return values * lax.rsqrt(mean_sq + 1e-06) * gain_vector.astype(jnp.float32)


def self_attend(queries, keys_all, values, head_count):
    row_count, model_width = queries.shape
    head_size = model_width // head_count
    queries = queries.reshape(row_count, head_count, head_size)
    keys_all = keys_all.reshape(-1, head_count, head_size)
    values = values.reshape(-1, head_count, head_size)
    scores = jnp.einsum(
        "shd,thd->hst", queries, keys_all, preferred_element_type=jnp.float32
    ) * head_size ** (-0.5)
    row_max = jnp.max(scores, axis=-1, keepdims=True)
    weights = jnp.exp(scores - row_max)
    soft_weights = (weights / jnp.sum(weights, axis=-1, keepdims=True)).astype(jnp.bfloat16)
    context = jnp.einsum("hst,thd->shd", soft_weights, values, preferred_element_type=jnp.float32)
    return context.reshape(row_count, model_width).astype(jnp.bfloat16)


def stage_orders():
    role_bits = lax.axis_size("role").bit_length() - 1
    dev_bits = lax.axis_size("dev").bit_length() - 1
    tops = list(range(dev_bits, dev_bits + role_bits))
    mids = list(range(dev_bits - 1, 0, -1))
    near, rest = mids[:2], mids[2:]
    return near + tops + rest, near + rest + tops, tops + rest + near


def swap(block, bit):
    count = lax.axis_size(AXES)
    return lax.ppermute(block, AXES, [(i, i ^ (1 << bit)) for i in range(count)])


def gather(shard, order):
    held = shard
    for bit in order[:-1]:
        held = jnp.concatenate([held, swap(held, bit)], axis=0)
    last = swap(held, order[-1])
    return [held, last, swap(held, 0), swap(last, 0)]


def source_device(slot, order, me):
    offset = jnp.zeros_like(slot)
    for place, bit in enumerate(list(order) + [0]):
        offset = offset + (((slot >> place) & 1) << bit)
    return offset ^ me


def column_order(order, me, width, shard_rows):
    wanted = lax.broadcasted_iota(jnp.int32, (1, width), 1)
    source = source_device(wanted // shard_rows, order, me) * shard_rows + wanted % shard_rows
    return (lax.broadcasted_iota(jnp.int32, (width, width), 0) == source).astype(jnp.bfloat16)


def exact_dot(left, right):
    return jnp.dot(left, right, preferred_element_type=jnp.float32).astype(jnp.bfloat16)


def shards(
    tokens,
    expert_ids,
    w_qkv,
    w_attn_out,
    gain_attn,
    gain_expert,
    router,
    expert_in,
    expert_out,
    capacity,
    swap_list,
):
    seq_len, model_width = tokens.shape
    shard_rows = w_qkv.shape[0]
    experts_all = router.shape[1]
    dev_count = lax.axis_size("dev")
    me = lax.axis_index(AXES)
    order_q, order_k, order_v = stage_orders()
    order_o = order_q

    chosen = expert_ids[:, 0]
    expert_range = jnp.arange(experts_all, dtype=jnp.int32)
    match = chosen[:, None] == expert_range[None, :]
    counts = jnp.sum(match.astype(jnp.int32), axis=0)

    pieces_q = gather(w_qkv[:, :model_width], order_q)
    pieces_k = gather(w_qkv[:, model_width : 2 * model_width], order_k)
    pieces_v = gather(w_qkv[:, 2 * model_width :], order_v)
    tail = -(-experts_all // LANES) * LANES
    count_block = jnp.zeros((shard_rows, tail), jnp.bfloat16)
    count_block = count_block.at[0, :experts_all].set(counts.astype(jnp.bfloat16))
    out_shard = jnp.concatenate([w_attn_out, count_block], axis=1)
    out_shard, _ = lax.optimization_barrier((out_shard, pieces_q[1]))
    pieces_o = gather(out_shard, order_o)

    residual = tokens.astype(jnp.float32)
    normed = rms_scale(residual, gain_attn).astype(jnp.bfloat16)
    mixer = jnp.concatenate(
        [column_order(o, me, model_width, shard_rows) for o in (order_q, order_k, order_v)], axis=1
    )
    normed_all = exact_dot(normed, mixer)
    parts = []
    for index, pieces in enumerate((pieces_q, pieces_k, pieces_v)):
        part = normed_all[:, index * model_width : (index + 1) * model_width]
        parts.append(exact_dot(part, jnp.concatenate(pieces, axis=0)))
    context = self_attend(*parts, HEADS)
    context = exact_dot(context, column_order(order_o, me, model_width, shard_rows))
    w_out = jnp.concatenate(pieces_o, axis=0)
    attended = jnp.dot(context, w_out[:, :model_width], preferred_element_type=jnp.float32)
    hidden = residual + attended
    normed_ffn = rms_scale(hidden, gain_expert).astype(jnp.bfloat16)
    logits = jnp.dot(normed_ffn, router, preferred_element_type=jnp.float32)
    gate = jax.nn.sigmoid(jnp.sum(jnp.where(match, logits, 0.0), axis=1))

    shard_index = jnp.arange(model_width, dtype=jnp.int32)
    lower = (source_device(shard_index // shard_rows, order_o, me) < me) & (
        shard_index % shard_rows == 0
    )
    counts_all = w_out[:, model_width : model_width + experts_all].astype(jnp.float32)
    before = jnp.sum(jnp.where(lower[:, None], counts_all, 0.0), axis=0).astype(jnp.int32)

    row_ids = lax.broadcasted_iota(jnp.int32, (seq_len, seq_len), 0)
    col_ids = lax.broadcasted_iota(jnp.int32, (seq_len, seq_len), 1)
    strict_lower = (col_ids < row_ids).astype(jnp.bfloat16)
    rank_table = jnp.dot(
        strict_lower, match.astype(jnp.bfloat16), preferred_element_type=jnp.float32
    )
    local_rank = jnp.sum(jnp.where(match, rank_table, 0.0), axis=1).astype(jnp.int32)
    position = local_rank + jnp.sum(jnp.where(match, before[None, :], 0), axis=1)
    flagged = jnp.any(swap_list[:, None] == jnp.arange(dev_count, dtype=jnp.int32)[None, :], axis=0)
    dev_index = expert_range % dev_count
    role_index = expert_range // dev_count
    flag_expert = jnp.any(
        (dev_index[:, None] == jnp.arange(dev_count, dtype=jnp.int32)[None, :]) & flagged[None, :],
        axis=1,
    )
    location = jnp.where(flag_expert, (1 - role_index) * dev_count + dev_index, expert_range)
    cap_expert = jnp.sum(
        jnp.where(location[:, None] == expert_range[None, :], capacity[None, :], 0), axis=1
    )
    limit = jnp.sum(jnp.where(match, cap_expert[None, :], 0), axis=1)
    kept = position < limit

    slot_rows = max(2, 2 * seq_len // experts_all)
    weight_in = expert_in[0]
    weight_out = expert_out[0]
    slot_index = chosen * slot_rows + local_rank
    buffer = (
        jnp.zeros((experts_all * slot_rows, model_width), jnp.bfloat16)
        .at[slot_index]
        .set(normed_ffn)
    )
    buffer = buffer.reshape(experts_all, slot_rows, model_width)
    received = lax.all_to_all(buffer, AXES, split_axis=0, concat_axis=0, tiled=True)
    flat_rows = received.reshape(-1, model_width)
    activ = jnp.maximum(
        jnp.dot(flat_rows, weight_in, preferred_element_type=jnp.float32), 0.0
    ).astype(jnp.bfloat16)
    produced = jnp.dot(activ, weight_out, preferred_element_type=jnp.float32).astype(jnp.bfloat16)
    returned = lax.all_to_all(
        produced.reshape(received.shape), AXES, split_axis=0, concat_axis=0, tiled=True
    )
    picked = returned.reshape(-1, model_width)[slot_index].astype(jnp.float32)
    mixed = hidden + jnp.where(kept, gate, 0.0)[:, None] * picked
    return mixed.astype(jnp.bfloat16)


def solution(mesh):
    rows = P(AXES, None)
    return jax.shard_map(
        shards,
        mesh=mesh,
        in_specs=(
            rows,
            rows,
            rows,
            rows,
            P(),
            P(),
            P(),
            P(AXES, None, None),
            P(AXES, None, None),
            P(),
            P(),
        ),
        out_specs=rows,
        check_vma=False,
    )
```

```python
import functools

import jax
import jax.numpy as jnp
from jax import lax
from jax.experimental import pallas as pl
from jax.experimental.pallas import tpu as pltpu
from jax.sharding import PartitionSpec as P


HEADS = 16
PARTS = 2
AXES = ("role", "dev")
LANES = 128
BF = jnp.bfloat16
F32 = jnp.float32
I32 = jnp.int32


def stage_orders():
    role_bits = lax.axis_size("role").bit_length() - 1
    dev_bits = lax.axis_size("dev").bit_length() - 1
    tops = list(range(dev_bits, dev_bits + role_bits))
    mids = list(range(dev_bits - 1, 0, -1))
    near, rest = mids[:2], mids[2:]
    return near + tops + rest, near + rest + tops, tops + rest + near


def swap(block, bit):
    count = lax.axis_size(AXES)
    return lax.ppermute(block, AXES, [(i, i ^ (1 << bit)) for i in range(count)])


def gather(shard, order):
    held = shard
    for bit in order[:-1]:
        held = jnp.concatenate([held, swap(held, bit)], axis=0)
    last = swap(held, order[-1])
    return [held, last, swap(held, 0), swap(last, 0)]


def source_device(slot, order, me):
    offset = jnp.zeros_like(slot)
    for place, bit in enumerate(list(order) + [0]):
        offset = offset + (((slot >> place) & 1) << bit)
    return offset ^ me


def column_order(order, me, width, shard_rows):
    wanted = lax.broadcasted_iota(I32, (1, width), 1)
    source = source_device(wanted // shard_rows, order, me) * shard_rows + wanted % shard_rows
    rows = lax.broadcasted_iota(I32, (width, width), 0)
    return jnp.where(rows == source, 1.0, 0.0).astype(BF)


def dot(left, right):
    return jnp.dot(left, right, preferred_element_type=F32)


def rms_scale(values, gain):
    mean_sq = jnp.mean(values * values, axis=-1, keepdims=True)
    return values * lax.rsqrt(mean_sq + 1e-06) * gain.astype(F32)


def call(body, out_shape, *operands, flops=0, in_specs=None, **kw):
    moved = sum(o.size * o.dtype.itemsize for o in operands)
    moved += sum(o.size * o.dtype.itemsize for o in jax.tree.leaves(out_shape))
    return pl.pallas_call(
        body,
        out_shape=out_shape,
        in_specs=in_specs or [pl.BlockSpec(memory_space=pltpu.VMEM)] * len(operands),
        cost_estimate=pl.CostEstimate(
            flops=int(flops), bytes_accessed=int(moved), transcendentals=0
        ),
        **kw,
    )(*operands)


def spot(shape, axis):
    return lax.broadcasted_iota(I32, shape, axis)


def index_body(slots, col_ref, row_ref, order_ref, undo_ref, chosen_ref, rank_ref, slot_ref, line_ref, count_ref):
    n, experts = col_ref.shape[0], count_ref.shape[1]
    ids_c, ids_r = col_ref[...], row_ref[...]
    match = jnp.where(ids_c == spot((n, experts), 1), 1.0, 0.0)
    match_t = jnp.where(ids_r == spot((experts, n), 0), 1.0, 0.0)
    down, across = spot((n, n), 0), spot((n, n), 1)
    rank_c = jnp.sum(
        match * dot(jnp.where(across < down, 1.0, 0.0).astype(BF), match.astype(BF)),
        axis=1,
        keepdims=True,
    )
    rank_r = jnp.sum(
        match_t * dot(match_t.astype(BF), jnp.where(down < across, 1.0, 0.0).astype(BF)),
        axis=0,
        keepdims=True,
    )
    count_r = jnp.sum(match, axis=0, keepdims=True)
    count_c = jnp.sum(match_t, axis=1, keepdims=True)
    e_down, e_across = spot((experts, experts), 0), spot((experts, experts), 1)
    first_r = jnp.sum(jnp.where(e_down < e_across, count_c, 0.0), axis=0, keepdims=True)
    first_c = jnp.sum(jnp.where(e_across < e_down, count_r, 0.0), axis=1, keepdims=True)
    sorted_c = (jnp.sum(match * first_r, axis=1, keepdims=True) + rank_c).astype(I32)
    sorted_r = (jnp.sum(match_t * first_c, axis=0, keepdims=True) + rank_r).astype(I32)
    place_c = lax.rem(sorted_c, PARTS) * (n // PARTS) + lax.div(sorted_c, PARTS)
    place_r = lax.rem(sorted_r, PARTS) * (n // PARTS) + lax.div(sorted_r, PARTS)
    order = place_r == down
    undo = place_c == across
    order_ref[...] = jnp.where(order, 1.0, 0.0).astype(BF)
    undo_ref[...] = jnp.where(undo, 1.0, 0.0).astype(BF)
    rank_ci, rank_ri = rank_c.astype(I32), rank_r.astype(I32)
    slot_c = (ids_c * slots + lax.div(rank_ci, PARTS)).astype(F32)
    slot_r = (ids_r * slots + lax.div(rank_ri, PARTS)).astype(F32)

    def column(line):
        return jnp.sum(jnp.where(order, line, 0.0), axis=1, keepdims=True).astype(I32)

    chosen_ref[...] = column(ids_r.astype(F32))
    rank_ref[...] = column(rank_r)
    slot_ref[...] = column(slot_r)
    line_ref[...] = jnp.sum(jnp.where(undo, slot_c, 0.0), axis=0, keepdims=True).astype(I32)
    count_ref[...] = count_r


def mix_qk_body(orders, shard_rows, me_ref, order_ref, tok_ref, gain_ref, res_ref, norm_ref, q_ref, k_ref, m_ref):
    width = tok_ref.shape[1]
    moved = dot(order_ref[...], tok_ref[...])
    res_ref[...] = moved.astype(BF)
    normed = rms_scale(moved, gain_ref[...]).astype(BF)
    norm_ref[...] = normed
    mixer = column_order(orders[0], me_ref[0], width, shard_rows)
    m_ref[...] = mixer
    q_ref[...] = dot(normed, mixer).astype(BF)
    k_ref[...] = dot(normed, column_order(orders[1], me_ref[0], width, shard_rows)).astype(BF)


def mix_v_body(order, shard_rows, me_ref, norm_ref, v_ref):
    mixer = column_order(order, me_ref[0], norm_ref.shape[1], shard_rows)
    v_ref[...] = dot(norm_ref[...], mixer).astype(BF)


def attend(queries, keys, values, head_size):
    scale = head_size ** (-0.5)
    pair = max(1, LANES // head_size)
    wide = pair * head_size
    rows, total = queries.shape
    lane = spot((rows, wide), 1) // head_size
    ones = jnp.ones((keys.shape[0], wide), BF)
    outs = []
    for start in range(0, total, wide):
        q = queries[:, start : start + wide]
        k = keys[:, start : start + wide]
        v = jnp.concatenate([values[:, start : start + wide], ones], axis=1)
        out = jnp.zeros((rows, wide), F32)
        for head in range(pair):
            own = lane == head
            scores = lax.dot_general(
                jnp.where(own, q, jnp.zeros_like(q)),
                k,
                (((1,), (1,)), ((), ())),
                preferred_element_type=F32,
            )
            top = jnp.max(scores, axis=1, keepdims=True)
            weights = jnp.exp((scores - top) * scale).astype(BF)
            both = dot(weights, v)
            out = jnp.where(own, both[:, :wide] / both[:, wide:], out)
        outs.append(out.astype(BF))
    return jnp.concatenate(outs, axis=1)


def project_body(head_size, pieces, *refs):
    xs, ws, outs = refs[:3], refs[3 : 3 + 3 * pieces], refs[3 + 3 * pieces :]
    ctx_ref, later_ref, k_ref, v_ref = outs
    made = []
    for which in range(3):
        total = None
        for piece in range(pieces):
            w = ws[which * pieces + piece]
            depth = w.shape[0]
            term = dot(xs[which][:, piece * depth : (piece + 1) * depth], w[...])
            total = term if total is None else total + term
        made.append(total.astype(BF))
    q, k, v = made
    part = ctx_ref.shape[0]
    k_ref[...] = k
    v_ref[...] = v
    later_ref[...] = q[part:]
    ctx_ref[...] = attend(q[:part], k, v, head_size)


def attend_body(head_size, q_ref, k_ref, v_ref, ctx_ref):
    ctx_ref[...] = attend(q_ref[...], k_ref[...], v_ref[...], head_size)


def post_body(slots, pieces, ctx_ref, mix_ref, *refs):
    ws, (res_ref, gain_ref, router_ref, chosen_ref, line_ref, hid_ref, gate_ref, buf_ref) = (
        refs[:pieces],
        refs[pieces:],
    )
    width = ctx_ref.shape[1]
    ctx = dot(ctx_ref[...], mix_ref[...]).astype(BF)
    hidden = res_ref[...].astype(F32)
    for piece, w in enumerate(ws):
        depth = w.shape[0]
        hidden = hidden + dot(ctx[:, piece * depth : (piece + 1) * depth], w[:, :width])
    hid_ref[...] = hidden
    normed = rms_scale(hidden, gain_ref[...]).astype(BF)
    logits = dot(normed, router_ref[...])
    own = chosen_ref[...] == spot(logits.shape, 1)
    gate_ref[...] = jax.nn.sigmoid(jnp.sum(jnp.where(own, logits, 0.0), axis=1, keepdims=True))
    take = jnp.where(spot((slots, ctx.shape[0]), 0) == line_ref[...], 1.0, 0.0).astype(BF)
    buf_ref[...] = dot(take, normed).astype(BF)


def combine_body(ret_ref, slot_ref, hid_ref, gate_ref, undo_ref, *refs):
    out_ref = refs[-1]
    rows, slots = hid_ref.shape[0], ret_ref.shape[0]
    take = jnp.where(spot((rows, slots), 1) == slot_ref[...], 1.0, 0.0).astype(BF)
    mixed = (hid_ref[...] + gate_ref[...] * dot(take, ret_ref[...])).astype(BF)
    out = dot(undo_ref[...], mixed)
    if len(refs) == 2:
        out = out + refs[0][...].astype(F32)
    out_ref[...] = out.astype(BF)


def shards(
    tokens,
    expert_ids,
    w_qkv,
    w_attn_out,
    gain_attn,
    gain_expert,
    router,
    expert_in,
    expert_out,
    capacity,
    swap_list,
):
    seq_len, width = tokens.shape
    shard_rows = w_qkv.shape[0]
    experts_all = router.shape[1]
    dev_count = lax.axis_size("dev")
    me = lax.axis_index(AXES)
    orders = stage_orders()
    order_o = orders[0]
    part = seq_len // PARTS
    bound = max(2, 2 * seq_len // experts_all)
    slots = -(-bound // PARTS)
    slot_count = experts_all * slots
    sds = jax.ShapeDtypeStruct

    pieces_q = gather(w_qkv[:, :width], orders[0])
    pieces_k = gather(w_qkv[:, width : 2 * width], orders[1])
    pieces_v = gather(w_qkv[:, 2 * width :], orders[2])

    order, undo, chosen, rank, slot, line, counts = call(
        functools.partial(index_body, slots),
        (
            sds((seq_len, seq_len), BF),
            sds((seq_len, seq_len), BF),
            sds((seq_len, 1), I32),
            sds((seq_len, 1), I32),
            sds((seq_len, 1), I32),
            sds((1, seq_len), I32),
            sds((1, experts_all), F32),
        ),
        expert_ids,
        expert_ids.reshape(1, seq_len),
        flops=4 * seq_len * seq_len * experts_all,
    )

    tail = -(-experts_all // LANES) * LANES
    count_block = jnp.pad(
        counts.astype(BF), ((0, shard_rows - 1), (0, tail - experts_all))
    )
    pieces_o = gather(jnp.concatenate([w_attn_out, count_block], axis=1), order_o)

    me_word = me.reshape(1).astype(I32)
    vm = pl.BlockSpec(memory_space=pltpu.VMEM)
    sm = pl.BlockSpec(memory_space=pltpu.SMEM)
    residual, normed, x_q, x_k, mixer = call(
        functools.partial(mix_qk_body, orders, shard_rows),
        (
            sds((seq_len, width), BF),
            sds((seq_len, width), BF),
            sds((seq_len, width), BF),
            sds((seq_len, width), BF),
            sds((width, width), BF),
        ),
        me_word,
        order,
        tokens,
        gain_attn.reshape(1, width),
        in_specs=[sm, vm, vm, vm],
        flops=4 * seq_len * width * width,
    )
    x_v = call(
        functools.partial(mix_v_body, orders[2], shard_rows),
        sds((seq_len, width), BF),
        me_word,
        normed,
        in_specs=[sm, vm],
        flops=2 * seq_len * width * width,
    )

    head_size = width // HEADS
    group = min(width, max(256, head_size))
    pieces = len(pieces_q)
    full = pl.BlockSpec((seq_len, width), lambda g: (0, 0))
    stripe = pl.BlockSpec((width // pieces, group), lambda g: (0, g))
    tall = pl.BlockSpec((seq_len, group), lambda g: (0, g))
    low = pl.BlockSpec((part, group), lambda g: (0, g))
    rest = pl.BlockSpec((seq_len - part, group), lambda g: (0, g))
    context, q_later, keys, values = call(
        functools.partial(project_body, head_size, pieces),
        (
            sds((part, width), BF),
            sds((seq_len - part, width), BF),
            sds((seq_len, width), BF),
            sds((seq_len, width), BF),
        ),
        x_q,
        x_k,
        x_v,
        *pieces_q,
        *pieces_k,
        *pieces_v,
        flops=6 * seq_len * width * width + 16 * part * seq_len * width,
        grid=(width // group,),
        in_specs=[full] * 3 + [stripe] * (3 * pieces),
        out_specs=[low, rest, tall, tall],
    )
    contexts = [context]
    for index in range(1, PARTS):
        q = q_later[(index - 1) * part : index * part]
        contexts.append(
            call(
                functools.partial(attend_body, head_size),
                sds((part, width), BF),
                q,
                keys,
                values,
                flops=16 * part * seq_len * width,
                grid=(width // group,),
                in_specs=[low, tall, tall],
                out_specs=low,
            )
        )

    shard_index = jnp.arange(width, dtype=I32)
    lower = (source_device(shard_index // shard_rows, order_o, me) < me) & (
        shard_index % shard_rows == 0
    )
    counts_all = jnp.concatenate([p[:, width : width + experts_all] for p in pieces_o], axis=0)
    before = jnp.sum(jnp.where(lower[:, None], counts_all.astype(F32), 0.0), axis=0).astype(I32)
    expert_range = jnp.arange(experts_all, dtype=I32)
    dev_range = jnp.arange(dev_count, dtype=I32)
    flagged = jnp.any(swap_list[:, None] == dev_range[None, :], axis=0)
    dev_index = expert_range % dev_count
    role_index = expert_range // dev_count
    flag_expert = jnp.any((dev_index[:, None] == dev_range[None, :]) & flagged[None, :], axis=1)
    location = jnp.where(flag_expert, (1 - role_index) * dev_count + dev_index, expert_range)
    room = jnp.sum(
        jnp.where(location[:, None] == expert_range[None, :], capacity[None, :], 0), axis=1
    )
    match = chosen == expert_range[None, :]
    left = jnp.sum(jnp.where(match, (room - before)[None, :], 0), axis=1, keepdims=True)
    kept = rank < left

    weight_in, weight_out = expert_in[0], expert_out[0]
    hiddens, gates, returned = [], [], []
    for index in range(PARTS):
        here = slice(index * part, (index + 1) * part)
        hidden, gate, buffer = call(
            functools.partial(post_body, slot_count, pieces),
            (
                sds((part, width), F32),
                sds((part, 1), F32),
                sds((slot_count, width), BF),
            ),
            contexts[index],
            mixer,
            *pieces_o,
            residual[here],
            gain_expert.reshape(1, width),
            router,
            chosen[here],
            line[:, here],
            flops=4 * part * width * width + 2 * slot_count * part * width,
        )
        hiddens.append(hidden)
        gates.append(gate)
        received = lax.all_to_all(buffer, AXES, split_axis=0, concat_axis=0, tiled=True)
        activ = jnp.maximum(dot(received, weight_in), 0.0).astype(BF)
        produced = dot(activ, weight_out).astype(BF)
        returned.append(
            lax.all_to_all(produced, AXES, split_axis=0, concat_axis=0, tiled=True)
        )
    out = None
    for index in range(PARTS):
        here = slice(index * part, (index + 1) * part)
        factor = jnp.where(kept[here], gates[index], 0.0)
        out = call(
            combine_body,
            sds((seq_len, width), BF),
            returned[index],
            slot[here],
            hiddens[index],
            factor,
            undo[:, here],
            *([] if out is None else [out]),
            flops=2 * part * width * (slot_count + seq_len),
        )
    return out


def solution(mesh):
    rows = P(AXES, None)

    return jax.shard_map(
        shards,
        mesh=mesh,
        in_specs=(
            rows,
            rows,
            rows,
            rows,
            P(),
            P(),
            P(),
            P(AXES, None, None),
            P(AXES, None, None),
            P(),
            P(),
        ),
        out_specs=rows,
        check_vma=False,
    )
```

```python
import functools
import math

import jax
import jax.numpy as jnp
from jax import lax
from jax.experimental import pallas as pl
from jax.experimental.pallas import tpu as pltpu
from jax.sharding import PartitionSpec as P


HEADS = 16
DEAL = 2
GRANT = 28 << 20
AXES = ("role", "dev")
LANES = 128
BF = jnp.bfloat16
F32 = jnp.float32
I32 = jnp.int32


def stage_orders():
    role_bits = lax.axis_size("role").bit_length() - 1
    dev_bits = lax.axis_size("dev").bit_length() - 1
    tops = list(range(dev_bits, dev_bits + role_bits))
    mids = list(range(dev_bits - 1, 0, -1))
    near, rest = mids[:2], mids[2:]
    return near + tops + rest, near + rest + tops, tops + rest + near


def swap(block, bit):
    count = lax.axis_size(AXES)
    return lax.ppermute(block, AXES, [(i, i ^ (1 << bit)) for i in range(count)])


def gather(shard, order):
    held = shard
    for bit in order[:-1]:
        held = jnp.concatenate([held, swap(held, bit)], axis=0)
    last = swap(held, order[-1])
    return [held, last, swap(held, 0), swap(last, 0)]


def gather_cut(shard, orders, shared, cut):
    held = shard
    for stage in range(shared):
        held = jnp.concatenate([held, swap(held, orders[0][stage])], axis=0)
    sides = []
    for part, order in zip((held[:, :cut], held[:, cut:]), orders):
        for bit in order[shared:-1]:
            moved = swap(part, bit)
            part = jnp.concatenate([part, moved], axis=0)
        sides.append([part, swap(part, order[-1])])
    return [[part, last, swap(part, 0), swap(last, 0)] for part, last in sides]


def source_device(slot, order, me):
    offset = jnp.zeros_like(slot)
    for place, bit in enumerate(list(order) + [0]):
        offset = offset + (((slot >> place) & 1) << bit)
    return offset ^ me


def offsets(order):
    made = [0]
    for bit in list(order) + [0]:
        made = made + [offset ^ (1 << bit) for offset in made]
    return made


def runs(order, target):
    held = offsets(order)
    places = [held.index(offset) for offset in offsets(target)]
    per = len(places) // 4
    stretches = []
    for start in range(0, len(places), per):
        made = []
        for place in places[start : start + per]:
            piece, first = place // per, place % per
            if made and made[-1][0] == piece and made[-1][1] + made[-1][2] == first:
                made[-1][2] += 1
            else:
                made.append([piece, first, 1])
        stretches.append(made)
    return stretches


def column_order(order, me, width, shard_rows):
    wanted = lax.broadcasted_iota(I32, (1, width), 1)
    source = source_device(wanted // shard_rows, order, me) * shard_rows + wanted % shard_rows
    rows = lax.broadcasted_iota(I32, (width, width), 0)
    return jnp.where(rows == source, 1.0, 0.0).astype(BF)


def dot(left, right):
    return jnp.dot(left, right, preferred_element_type=F32)


def rms_scale(values, gain):
    mean_sq = jnp.mean(values * values, axis=-1, keepdims=True)
    return values * lax.rsqrt(mean_sq + 1e-06) * gain.astype(F32)


def far(value):
    return pltpu.with_memory_space_constraint(value, pltpu.HBM)


def near(value):
    return pltpu.with_memory_space_constraint(value, pltpu.VMEM)


def call(body, out_shape, *operands, flops=0, in_specs=None, grant=None, **kw):
    leaves = list(operands) + jax.tree.leaves(out_shape)
    moved = sum(math.prod(leaf.shape) * leaf.dtype.itemsize for leaf in leaves)
    return pl.pallas_call(
        body,
        out_shape=out_shape,
        compiler_params=pltpu.CompilerParams(vmem_limit_bytes=grant),
        in_specs=in_specs or [pl.BlockSpec(memory_space=pltpu.VMEM)] * len(operands),
        cost_estimate=pl.CostEstimate(
            flops=int(flops), bytes_accessed=int(moved), transcendentals=0
        ),
        **kw,
    )(*operands)


def spot(shape, axis):
    return lax.broadcasted_iota(I32, shape, axis)


def dealt(rows):
    return rows // DEAL, rows - rows // DEAL


def index_body(slots, experts, row_ref, *outs):
    n = row_ref.shape[1]
    first_rows = dealt(n)[0]
    down, across = spot((n, n), 0), spot((n, n), 1)
    ids_r = row_ref[...].astype(F32)
    ids_c = jnp.sum(jnp.where(down == across, ids_r, 0.0), axis=1, keepdims=True)
    match = jnp.where(ids_c.astype(I32) == spot((n, experts), 1), 1.0, 0.0)
    match_t = jnp.where(row_ref[...] == spot((experts, n), 0), 1.0, 0.0)
    rank_c = jnp.sum(
        match * dot(jnp.where(across < down, 1.0, 0.0).astype(BF), match.astype(BF)),
        axis=1,
        keepdims=True,
    )
    rank_r = jnp.sum(
        match_t * dot(match_t.astype(BF), jnp.where(down < across, 1.0, 0.0).astype(BF)),
        axis=0,
        keepdims=True,
    )
    count_r = jnp.sum(match, axis=0, keepdims=True)
    count_c = jnp.sum(match_t, axis=1, keepdims=True)
    e_down, e_across = spot((experts, experts), 0), spot((experts, experts), 1)
    first_r = jnp.sum(jnp.where(e_down < e_across, count_c, 0.0), axis=0, keepdims=True)
    first_c = jnp.sum(jnp.where(e_across < e_down, count_r, 0.0), axis=1, keepdims=True)
    start_c = jnp.sum(match * first_r, axis=1, keepdims=True)
    start_r = jnp.sum(match_t * first_c, axis=0, keepdims=True)

    def places(ids, start, rank):
        ids, start, rank = ids.astype(I32), start.astype(I32), rank.astype(I32)
        at = start + rank
        turn, left = lax.div(at, DEAL), lax.rem(at, DEAL)
        early = left == 0
        place = jnp.where(early, turn, first_rows + turn * (DEAL - 1) + left - 1)
        ahead = lax.div(at + (DEAL - 1), DEAL) - lax.div(start + (DEAL - 1), DEAL)
        slot = jnp.where(early, ids * slots[0] + ahead, ids * slots[1] + rank - ahead)
        return place, slot.astype(F32)

    place_c, slot_c = places(ids_c, start_c, rank_c)
    place_r, slot_r = places(ids_r, start_r, rank_r)
    order = place_r == down
    undo = place_c == across
    order_ref, outs = outs[0], outs[1:]
    order_ref[...] = jnp.where(order, 1.0, 0.0).astype(BF)
    undone = jnp.where(undo, 1.0, 0.0).astype(BF)

    def column(line):
        return jnp.sum(jnp.where(order, line, 0.0), axis=1, keepdims=True).astype(I32)

    columns = [column(ids_r), column(rank_r), column(slot_r)]
    line = jnp.sum(jnp.where(undo, slot_c, 0.0), axis=0, keepdims=True).astype(I32)
    for index, (low, high) in enumerate(((0, first_rows), (first_rows, n))):
        undo_ref, chosen_ref, rank_ref, slot_ref, line_ref = outs[index * 5 : index * 5 + 5]
        undo_ref[...] = undone[:, low:high]
        for ref, made in zip((chosen_ref, rank_ref, slot_ref), columns):
            ref[...] = made[low:high]
        line_ref[...] = line[:, low:high]


def mix_body(order, shard_rows, me_ref, order_ref, tok_ref, gain_ref, res0_ref, res1_ref, x0_ref, x1_ref):
    width = tok_ref.shape[1]
    moved = dot(order_ref[...], tok_ref[...])
    first_rows = res0_ref.shape[0]
    res0_ref[...] = moved[:first_rows].astype(BF)
    res1_ref[...] = moved[first_rows:].astype(BF)
    normed = rms_scale(moved, gain_ref[...].reshape(1, width)).astype(BF)
    mixer = column_order(order, me_ref[0], width, shard_rows)
    mixed = dot(normed, mixer).astype(BF)
    x0_ref[...] = mixed[:first_rows]
    x1_ref[...] = mixed[first_rows:]


def attend(queries, keys, values, head_size):
    scale = head_size ** (-0.5)
    pair = max(1, LANES // head_size)
    wide = pair * head_size
    rows, total = queries.shape
    lane = spot((rows, wide), 1) // head_size
    ones = jnp.ones((keys.shape[0], wide), BF)
    outs = []
    for start in range(0, total, wide):
        q = queries[:, start : start + wide]
        k = keys[:, start : start + wide]
        v = jnp.concatenate([values[:, start : start + wide], ones], axis=1)
        stacked = jnp.concatenate(
            [jnp.where(lane == head, q, jnp.zeros_like(q)) for head in range(pair)], axis=0
        )
        scores = lax.dot_general(
            stacked, k, (((1,), (1,)), ((), ())), preferred_element_type=F32
        )
        top = jnp.max(scores, axis=1, keepdims=True)
        both = dot(jnp.exp((scores - top) * scale).astype(BF), v)
        ratio = both[:, :wide] / both[:, wide:]
        out = ratio[:rows]
        for head in range(1, pair):
            out = jnp.where(lane == head, ratio[head * rows : (head + 1) * rows], out)
        outs.append(out.astype(BF))
    return jnp.concatenate(outs, axis=1)


def times(x, pieces, stretches, shard_rows):
    total = None
    for index, stretch in enumerate(stretches):
        depth = shard_rows * sum(shards for _, _, shards in stretch)
        taken = [
            pieces[piece][first * shard_rows : (first + shards) * shard_rows, :]
            for piece, first, shards in stretch
        ]
        w = taken[0] if len(taken) == 1 else jnp.concatenate(taken, axis=0)
        term = dot(x[:, index * depth : (index + 1) * depth], w)
        total = term if total is None else total + term
    return total


def project_body(head_size, shard_rows, stretches, x0_ref, x1_ref, *refs):
    ws, (ctx_ref, k_ref, v_ref) = refs[:-3], refs[-3:]
    count = len(ws) // 3
    x0 = x0_ref[...]
    x = jnp.concatenate([x0, x1_ref[...]], axis=0)
    k = times(x, ws[count : 2 * count], stretches[1], shard_rows).astype(BF)
    v = times(x, ws[2 * count :], stretches[2], shard_rows).astype(BF)
    q = times(x0, ws[:count], stretches[0], shard_rows).astype(BF)
    k_ref[...] = k
    v_ref[...] = v
    ctx_ref[...] = attend(q, k, v, head_size)


def attend_body(head_size, shard_rows, stretches, x_ref, k_ref, v_ref, *refs):
    ws, ctx_ref = refs[:-1], refs[-1]
    q = times(x_ref[...], ws, stretches, shard_rows).astype(BF)
    ctx_ref[...] = attend(q, k_ref[...], v_ref[...], head_size)


def place_rows(shard_rows, orders, me, pieces, whole_ref):
    half = whole_ref.shape[1] // 2
    for side, order in enumerate(orders):
        held = offsets(order)
        per = len(held) // 4
        for place, offset in enumerate(held):
            at = pl.multiple_of((me ^ offset) * shard_rows, shard_rows)
            first = (place % per) * shard_rows
            whole_ref[pl.ds(at, shard_rows), side * half : (side + 1) * half] = pieces[
                side * 4 + place // per
            ][first : first + shard_rows, :half]


def post_rows(ctx, res, w, gain_ref, router_ref, chosen_ref, line_ref, hid_ref, buf_ref, sent=None):
    width = ctx.shape[1]
    hidden = res.astype(F32) + dot(ctx, w)
    hid_ref[:, :width] = hidden
    normed = rms_scale(hidden, gain_ref[...].reshape(1, width)).astype(BF)
    logits = lax.dot_general(
        normed, router_ref[...], (((1,), (1,)), ((), ())), preferred_element_type=F32
    )
    own = chosen_ref[...] == spot(logits.shape, 1)
    gate = jax.nn.sigmoid(jnp.sum(jnp.where(own, logits, 0.0), axis=1, keepdims=True))
    hid_ref[:, width:] = jnp.broadcast_to(gate, (hidden.shape[0], LANES))
    if sent is not None:
        sent.start()
    take = spot((buf_ref.shape[0], normed.shape[0]), 0) == line_ref[...]
    buf_ref[...] = dot(jnp.where(take, 1.0, 0.0).astype(BF), normed).astype(BF)


def post_first_body(shard_rows, orders, me_ref, *refs):
    pieces, (ctx_ref, res_ref, *small) = refs[:8], refs[8:14]
    hid_ref, buf_ref, w_ref, w_s, hid_s, sem = refs[14:]
    place_rows(shard_rows, orders, me_ref[0], pieces, w_s)
    kept = pltpu.make_async_copy(w_s, w_ref, sem.at[0])
    kept.start()
    sent = pltpu.make_async_copy(hid_s, hid_ref, sem.at[1])
    post_rows(ctx_ref[...], res_ref[...], w_s[...], *small, hid_s, buf_ref, sent)
    kept.wait()
    sent.wait()


def post_later_body(w_ref, ctx_ref, res_ref, *refs):
    post_rows(ctx_ref[...], res_ref[...], w_ref[...], *refs)


def moved(undo, values):
    total = None
    for _ in range(3):
        part = values.astype(BF)
        values = values - part.astype(F32)
        term = dot(undo, part)
        total = term if total is None else total + term
    return total


def settle_body(ret_ref, left_ref, *refs):
    sides, (total_ref, pick_ref, factor_ref) = (refs[:5], refs[5:10]), refs[10:]
    width = total_ref.shape[1]
    hidden = []
    for index, (hid, undo, slot, chosen, rank) in enumerate(sides):
        rows, slots = undo.shape[1], (ret_ref.shape[0], pick_ref.shape[1])[index]
        own = chosen[...] == spot((rows, left_ref.shape[1]), 1)
        left = jnp.sum(jnp.where(own, left_ref[...], 0.0), axis=1, keepdims=True)
        factor = jnp.where(rank[...].astype(F32) < left, hid[:, width:], 0.0)
        factor = moved(undo[...], factor)
        take = jnp.where(spot((rows, slots), 1) == slot[...], 1.0, 0.0).astype(BF)
        pick = dot(undo[...], take).astype(BF)
        hidden.append(moved(undo[...], hid[:, :width]))
        if index == 0:
            total_ref[...] = hidden[0] + factor[:, :1] * dot(pick, ret_ref[...])
        else:
            total_ref[...] = total_ref[...] + hidden[1]
            pick_ref[...] = pick
            factor_ref[...] = factor


def finish_body(ret_ref, total_ref, pick_ref, factor_ref, out_ref, out_s, sem):
    factor = factor_ref[:, :1]
    width = total_ref.shape[1]
    step = width // 4
    sent = []
    for index in range(4):
        here = slice(index * step, (index + 1) * step)
        picked = factor * dot(pick_ref[...], ret_ref[:, here])
        out_s[:, here] = (total_ref[:, here] + picked).astype(BF)
        sent.append(
            pltpu.make_async_copy(
                out_s.at[:, pl.ds(index * step, step)],
                out_ref.at[:, pl.ds(index * step, step)],
                sem.at[index],
            )
        )
        sent[-1].start()
    for copy in sent:
        copy.wait()


def shards(
    tokens,
    expert_ids,
    w_qkv,
    w_attn_out,
    gain_attn,
    gain_expert,
    router,
    expert_in,
    expert_out,
    capacity,
    swap_list,
):
    seq_len, width = tokens.shape
    shard_rows = w_qkv.shape[0]
    experts_all = router.shape[1]
    dev_count = lax.axis_size("dev")
    me = lax.axis_index(AXES)
    orders = stage_orders()
    order_o = orders[0]
    parts = dealt(seq_len)
    bound = max(2, 2 * seq_len // experts_all)
    slots = (-(-bound // DEAL), bound - bound // DEAL)
    sds = jax.ShapeDtypeStruct

    pieces_q = gather(w_qkv[:, :width], orders[0])
    pieces_k = gather(w_qkv[:, width : 2 * width], orders[1])
    pieces_v = gather(w_qkv[:, 2 * width :], orders[2])

    shapes = [sds((seq_len, seq_len), BF)]
    for rows in parts:
        shapes += [sds((seq_len, rows), BF)] + [sds((rows, 1), I32)] * 3 + [sds((1, rows), I32)]
    order, *made = call(
        functools.partial(index_body, slots, experts_all),
        tuple(shapes),
        expert_ids.reshape(1, seq_len),
        flops=4 * seq_len * seq_len * experts_all,
    )
    undo, chosen, rank, slot, line = ([made[k], made[k + 5]] for k in range(5))

    tail = -(-experts_all // LANES) * LANES
    named = expert_ids == jnp.arange(tail, dtype=I32)[None, :]
    counts = jnp.sum(named.astype(F32), axis=0, keepdims=True).astype(BF)
    count_block = jnp.pad(counts, ((0, shard_rows - 1), (0, 0)))
    cut = width // 2
    shared = min(2, len(order_o) - 1)
    pieces_o = gather_cut(
        jnp.concatenate([w_attn_out, count_block], axis=1), orders[:2], shared, cut
    )

    me_word = me.reshape(1).astype(I32)
    vm = pl.BlockSpec(memory_space=pltpu.VMEM)
    sm = pl.BlockSpec(memory_space=pltpu.SMEM)
    hbm = pl.BlockSpec(memory_space=pl.ANY)
    made = call(
        functools.partial(mix_body, order_o, shard_rows),
        (
            sds((parts[0], width), BF),
            sds((parts[1], width), BF),
            sds((parts[0], width), BF),
            sds((parts[1], width), BF),
        ),
        me_word,
        order,
        tokens,
        gain_attn,
        in_specs=[sm, vm, vm, vm],
        flops=2 * seq_len * width * width,
    )
    residual, x = list(made[:2]), list(made[2:])

    head_size = width // HEADS
    group = min(width, max(256, head_size))
    pieces = len(pieces_q)
    stretches = [runs(o, order_o) for o in orders]

    def whole(*shape):
        return pl.BlockSpec(shape, lambda g: (0, 0))

    def striped(height):
        return pl.BlockSpec((height, group), lambda g: (0, g))

    stripes = [striped(width // pieces)] * pieces
    tall = striped(seq_len)
    context, keys, values = call(
        functools.partial(project_body, head_size, shard_rows, stretches),
        (
            pltpu.VMEM((parts[0], width), BF),
            pltpu.HBM((seq_len, width), BF),
            pltpu.HBM((seq_len, width), BF),
        ),
        *[far(value) for value in x + pieces_q + pieces_k + pieces_v],
        grant=GRANT,
        flops=5 * seq_len * width * width + 16 * parts[0] * seq_len * width,
        grid=(width // group,),
        in_specs=[whole(parts[0], width), whole(parts[1], width)] + stripes * 3,
        out_specs=[striped(parts[0]), tall, tall],
    )
    context_later = call(
        functools.partial(attend_body, head_size, shard_rows, stretches[0]),
        sds((parts[1], width), BF),
        x[1],
        keys,
        values,
        *pieces_q,
        flops=16 * parts[1] * seq_len * width + 2 * parts[1] * width * width,
        grid=(width // group,),
        in_specs=[whole(parts[1], width), tall, tall] + stripes,
        out_specs=striped(parts[1]),
    )
    contexts = [context, context_later]

    shard_index = jnp.arange(width, dtype=I32)
    lower = (source_device(shard_index // shard_rows, orders[1], me) < me) & (
        shard_index % shard_rows == 0
    )
    counts_all = jnp.concatenate(
        [p[:, width - cut : width - cut + experts_all] for p in pieces_o[1]], axis=0
    )
    before = jnp.sum(jnp.where(lower[:, None], counts_all.astype(F32), 0.0), axis=0).astype(I32)
    expert_range = jnp.arange(experts_all, dtype=I32)
    dev_range = jnp.arange(dev_count, dtype=I32)
    flagged = jnp.any(swap_list[:, None] == dev_range[None, :], axis=0)
    dev_index = expert_range % dev_count
    role_index = expert_range // dev_count
    flag_expert = jnp.any((dev_index[:, None] == dev_range[None, :]) & flagged[None, :], axis=1)
    location = jnp.where(flag_expert, (1 - role_index) * dev_count + dev_index, expert_range)
    room = jnp.sum(
        jnp.where(location[:, None] == expert_range[None, :], capacity[None, :], 0), axis=1
    )
    left = (room - before).astype(F32).reshape(1, experts_all)

    weight_in, weight_out = expert_in[0], expert_out[0]
    hiddens, returned = [], []
    for index, rows in enumerate(parts):
        slot_count = experts_all * slots[index]
        small = (gain_expert, router.T, chosen[index], line[index])
        cost = 2 * rows * width * width + 2 * slot_count * rows * width
        if index == 0:
            hidden, buffer, w_placed = call(
                functools.partial(post_first_body, shard_rows, orders[:2]),
                (
                    pltpu.HBM((rows, width + LANES), F32),
                    pltpu.VMEM((slot_count, width), BF),
                    pltpu.HBM((width, width), BF),
                ),
                me_word,
                *[near(piece) for piece in pieces_o[0] + pieces_o[1]],
                *[near(value) for value in (contexts[0], residual[0], *small)],
                flops=cost,
                grant=GRANT,
                in_specs=[sm] + [vm] * 14,
                out_specs=[hbm, vm, hbm],
                scratch_shapes=[
                    pltpu.VMEM((width, width), BF),
                    pltpu.VMEM((rows, width + LANES), F32),
                    pltpu.SemaphoreType.DMA((2,)),
                ],
            )
        else:
            hidden, buffer = call(
                post_later_body,
                (
                    sds((rows, width + LANES), F32),
                    sds((slot_count, width), BF),
                ),
                w_placed,
                contexts[index],
                residual[index],
                *small,
                flops=cost,
            )
        hiddens.append(hidden)
        received = lax.all_to_all(buffer, AXES, split_axis=0, concat_axis=0, tiled=True)
        activ = jnp.maximum(dot(received, weight_in), 0.0).astype(BF)
        produced = dot(activ, weight_out).astype(BF)
        returned.append(
            lax.all_to_all(produced, AXES, split_axis=0, concat_axis=0, tiled=True)
        )
    sides = []
    for index in range(len(parts)):
        sides += [hiddens[index], undo[index], slot[index], chosen[index], rank[index]]
    later_slots = experts_all * slots[1]
    total, pick, factor = call(
        settle_body,
        (
            pltpu.VMEM((seq_len, width), F32),
            pltpu.VMEM((seq_len, later_slots), BF),
            pltpu.VMEM((seq_len, LANES), F32),
        ),
        returned[0],
        left,
        *[far(side) for side in sides],
        flops=8 * seq_len * seq_len * width,
        grant=GRANT,
    )
    return call(
        finish_body,
        sds((seq_len, width), BF),
        near(returned[1]),
        near(total),
        near(pick),
        near(factor),
        flops=2 * seq_len * width * later_slots,
        grant=GRANT,
        out_specs=hbm,
        scratch_shapes=[pltpu.VMEM((seq_len, width), BF), pltpu.SemaphoreType.DMA((4,))],
    )


def solution(mesh):
    rows = P(AXES, None)

    return jax.shard_map(
        shards,
        mesh=mesh,
        in_specs=(
            rows,
            rows,
            rows,
            rows,
            P(),
            P(),
            P(),
            P(AXES, None, None),
            P(AXES, None, None),
            P(),
            P(),
        ),
        out_specs=rows,
        check_vma=False,
    )
```

```python
import functools
import math

import jax
import jax.numpy as jnp
from jax import lax
from jax.experimental import pallas as pl
from jax.experimental.pallas import tpu as pltpu
from jax.sharding import PartitionSpec as P


HEADS = 16
DEAL = 2
GRANT = 28 << 20
AXES = ("role", "dev")
LANES = 128
BF = jnp.bfloat16
F32 = jnp.float32
I32 = jnp.int32


def stage_orders():
    role_bits = lax.axis_size("role").bit_length() - 1
    dev_bits = lax.axis_size("dev").bit_length() - 1
    tops = list(range(dev_bits, dev_bits + role_bits))
    mids = list(range(dev_bits - 1, 0, -1))
    near, rest = mids[:2], mids[2:]
    return near + tops + rest, near + rest + tops, tops + rest + near


def swap(block, bit):
    count = lax.axis_size(AXES)
    return lax.ppermute(block, AXES, [(i, i ^ (1 << bit)) for i in range(count)])


def gather(shard, order):
    held = shard
    for bit in order[:-1]:
        held = jnp.concatenate([held, swap(held, bit)], axis=0)
    last = swap(held, order[-1])
    return [held, last, swap(held, 0), swap(last, 0)]


def gather_cut(shard, orders, shared, cut):
    held = shard
    for stage in range(shared):
        held = jnp.concatenate([held, swap(held, orders[0][stage])], axis=0)
    sides = []
    for part, order in zip((held[:, :cut], held[:, cut:]), orders):
        for bit in order[shared:-1]:
            moved = swap(part, bit)
            part = jnp.concatenate([part, moved], axis=0)
        sides.append([part, swap(part, order[-1])])
    return [[part, last, swap(part, 0), swap(last, 0)] for part, last in sides]


def source_device(slot, order, me):
    offset = jnp.zeros_like(slot)
    for place, bit in enumerate(list(order) + [0]):
        offset = offset + (((slot >> place) & 1) << bit)
    return offset ^ me


def offsets(order):
    made = [0]
    for bit in list(order) + [0]:
        made = made + [offset ^ (1 << bit) for offset in made]
    return made


def runs(order, target):
    held = offsets(order)
    places = [held.index(offset) for offset in offsets(target)]
    per = len(places) // 4
    stretches = []
    for start in range(0, len(places), per):
        made = []
        for place in places[start : start + per]:
            piece, first = place // per, place % per
            if made and made[-1][0] == piece and made[-1][1] + made[-1][2] == first:
                made[-1][2] += 1
            else:
                made.append([piece, first, 1])
        stretches.append(made)
    return stretches


def column_order(order, me, width, shard_rows):
    wanted = lax.broadcasted_iota(I32, (1, width), 1)
    source = source_device(wanted // shard_rows, order, me) * shard_rows + wanted % shard_rows
    rows = lax.broadcasted_iota(I32, (width, width), 0)
    return jnp.where(rows == source, 1.0, 0.0).astype(BF)


def dot(left, right):
    return jnp.dot(left, right, preferred_element_type=F32)


def rms_scale(values, gain):
    mean_sq = jnp.mean(values * values, axis=-1, keepdims=True)
    return values * lax.rsqrt(mean_sq + 1e-06) * gain.astype(F32)


def far(value):
    return pltpu.with_memory_space_constraint(value, pltpu.HBM)


def near(value):
    return pltpu.with_memory_space_constraint(value, pltpu.VMEM)


def call(body, out_shape, *operands, flops=0, in_specs=None, grant=None, **kw):
    leaves = list(operands) + jax.tree.leaves(out_shape)
    moved = sum(math.prod(leaf.shape) * leaf.dtype.itemsize for leaf in leaves)
    return pl.pallas_call(
        body,
        out_shape=out_shape,
        compiler_params=pltpu.CompilerParams(vmem_limit_bytes=grant),
        in_specs=in_specs or [pl.BlockSpec(memory_space=pltpu.VMEM)] * len(operands),
        cost_estimate=pl.CostEstimate(
            flops=int(flops), bytes_accessed=int(moved), transcendentals=0
        ),
        **kw,
    )(*operands)


def spot(shape, axis):
    return lax.broadcasted_iota(I32, shape, axis)


def dealt(rows):
    return rows // DEAL, rows - rows // DEAL


def index_body(slots, experts, row_ref, *outs):
    n = row_ref.shape[1]
    first_rows = dealt(n)[0]
    down, across = spot((n, n), 0), spot((n, n), 1)
    ids_r = row_ref[...].astype(F32)
    ids_c = jnp.sum(jnp.where(down == across, ids_r, 0.0), axis=1, keepdims=True)
    match = jnp.where(ids_c.astype(I32) == spot((n, experts), 1), 1.0, 0.0)
    match_t = jnp.where(row_ref[...] == spot((experts, n), 0), 1.0, 0.0)
    rank_c = jnp.sum(
        match * dot(jnp.where(across < down, 1.0, 0.0).astype(BF), match.astype(BF)),
        axis=1,
        keepdims=True,
    )
    rank_r = jnp.sum(
        match_t * dot(match_t.astype(BF), jnp.where(down < across, 1.0, 0.0).astype(BF)),
        axis=0,
        keepdims=True,
    )
    count_r = jnp.sum(match, axis=0, keepdims=True)
    count_c = jnp.sum(match_t, axis=1, keepdims=True)
    e_down, e_across = spot((experts, experts), 0), spot((experts, experts), 1)
    first_r = jnp.sum(jnp.where(e_down < e_across, count_c, 0.0), axis=0, keepdims=True)
    first_c = jnp.sum(jnp.where(e_across < e_down, count_r, 0.0), axis=1, keepdims=True)
    start_c = jnp.sum(match * first_r, axis=1, keepdims=True)
    start_r = jnp.sum(match_t * first_c, axis=0, keepdims=True)

    def places(ids, start, rank):
        ids, start, rank = ids.astype(I32), start.astype(I32), rank.astype(I32)
        at = start + rank
        turn, left = lax.div(at, DEAL), lax.rem(at, DEAL)
        early = left == 0
        place = jnp.where(early, turn, first_rows + turn * (DEAL - 1) + left - 1)
        ahead = lax.div(at + (DEAL - 1), DEAL) - lax.div(start + (DEAL - 1), DEAL)
        slot = jnp.where(early, ids * slots[0] + ahead, ids * slots[1] + rank - ahead)
        return place, slot.astype(F32)

    place_c, slot_c = places(ids_c, start_c, rank_c)
    place_r, slot_r = places(ids_r, start_r, rank_r)
    order = place_r == down
    undo = place_c == across
    order_ref, outs = outs[0], outs[1:]
    order_ref[...] = jnp.where(order, 1.0, 0.0).astype(BF)
    undone = jnp.where(undo, 1.0, 0.0).astype(BF)

    def column(line):
        return jnp.sum(jnp.where(order, line, 0.0), axis=1, keepdims=True).astype(I32)

    columns = [column(ids_r), column(rank_r), column(slot_r)]
    line = jnp.sum(jnp.where(undo, slot_c, 0.0), axis=0, keepdims=True).astype(I32)
    for index, (low, high) in enumerate(((0, first_rows), (first_rows, n))):
        undo_ref, chosen_ref, rank_ref, slot_ref, line_ref = outs[index * 5 : index * 5 + 5]
        undo_ref[...] = undone[:, low:high]
        for ref, made in zip((chosen_ref, rank_ref, slot_ref), columns):
            ref[...] = made[low:high]
        line_ref[...] = line[:, low:high]


def mix_body(order, shard_rows, me_ref, order_ref, tok_ref, gain_ref, res0_ref, res1_ref, x0_ref, x1_ref):
    width = tok_ref.shape[1]
    moved = dot(order_ref[...], tok_ref[...])
    first_rows = res0_ref.shape[0]
    res0_ref[...] = moved[:first_rows].astype(BF)
    res1_ref[...] = moved[first_rows:].astype(BF)
    normed = rms_scale(moved, gain_ref[...].reshape(1, width)).astype(BF)
    mixer = column_order(order, me_ref[0], width, shard_rows)
    mixed = dot(normed, mixer).astype(BF)
    x0_ref[...] = mixed[:first_rows]
    x1_ref[...] = mixed[first_rows:]


def attend(queries, keys, values, head_size, ahead=False):
    scale = head_size ** (-0.5)
    pair = max(1, LANES // head_size)
    wide = pair * head_size
    rows, total = queries.shape
    lane = spot((rows, wide), 1) // head_size
    ones = jnp.ones((keys.shape[0], wide), BF)

    def score(start):
        q = queries[:, start : start + wide]
        stacked = jnp.concatenate(
            [jnp.where(lane == head, q, jnp.zeros_like(q)) for head in range(pair)], axis=0
        )
        return lax.dot_general(
            stacked,
            keys[:, start : start + wide],
            (((1,), (1,)), ((), ())),
            preferred_element_type=F32,
        )

    def mix(start, scores):
        v = jnp.concatenate([values[:, start : start + wide], ones], axis=1)
        top = jnp.max(scores, axis=1, keepdims=True)
        both = dot(jnp.exp((scores - top) * scale).astype(BF), v)
        ratio = both[:, :wide] / both[:, wide:]
        out = ratio[:rows]
        for head in range(1, pair):
            out = jnp.where(lane == head, ratio[head * rows : (head + 1) * rows], out)
        return out.astype(BF)

    starts = range(0, total, wide)
    if ahead:
        made = [score(start) for start in starts]
        outs = [mix(start, scores) for start, scores in zip(starts, made)]
    else:
        outs = [mix(start, score(start)) for start in starts]
    return jnp.concatenate(outs, axis=1)


def times(x, pieces, stretches, shard_rows):
    total = None
    for index, stretch in enumerate(stretches):
        depth = shard_rows * sum(shards for _, _, shards in stretch)
        taken = [
            pieces[piece][first * shard_rows : (first + shards) * shard_rows, :]
            for piece, first, shards in stretch
        ]
        w = taken[0] if len(taken) == 1 else jnp.concatenate(taken, axis=0)
        term = dot(x[:, index * depth : (index + 1) * depth], w)
        total = term if total is None else total + term
    return total


def project_body(head_size, shard_rows, stretches, x0_ref, x1_ref, *refs):
    ws, (ctx_ref, k_ref, v_ref) = refs[:-3], refs[-3:]
    count = len(ws) // 3
    x0 = x0_ref[...]
    x = jnp.concatenate([x0, x1_ref[...]], axis=0)
    k = times(x, ws[count : 2 * count], stretches[1], shard_rows).astype(BF)
    v = times(x, ws[2 * count :], stretches[2], shard_rows).astype(BF)
    q = times(x0, ws[:count], stretches[0], shard_rows).astype(BF)
    k_ref[...] = k
    v_ref[...] = v
    ctx_ref[...] = attend(q, k, v, head_size)


def attend_body(head_size, shard_rows, stretches, x_ref, k_ref, v_ref, *refs):
    ws, ctx_ref = refs[:-1], refs[-1]
    q = times(x_ref[...], ws, stretches, shard_rows).astype(BF)
    ctx_ref[...] = attend(q, k_ref[...], v_ref[...], head_size, ahead=True)


def place_rows(shard_rows, orders, me, pieces, whole_ref):
    half = whole_ref.shape[1] // 2
    for side, order in enumerate(orders):
        held = offsets(order)
        per = len(held) // 4
        for place, offset in enumerate(held):
            at = pl.multiple_of((me ^ offset) * shard_rows, shard_rows)
            first = (place % per) * shard_rows
            whole_ref[pl.ds(at, shard_rows), side * half : (side + 1) * half] = pieces[
                side * 4 + place // per
            ][first : first + shard_rows, :half]


def post_rows(ctx, res, w, gain_ref, router_ref, chosen_ref, line_ref, hid_ref, buf_ref, sent=None):
    width = ctx.shape[1]
    hidden = res.astype(F32) + dot(ctx, w)
    hid_ref[:, :width] = hidden
    normed = rms_scale(hidden, gain_ref[...].reshape(1, width)).astype(BF)
    logits = lax.dot_general(
        normed, router_ref[...], (((1,), (1,)), ((), ())), preferred_element_type=F32
    )
    own = chosen_ref[...] == spot(logits.shape, 1)
    gate = jax.nn.sigmoid(jnp.sum(jnp.where(own, logits, 0.0), axis=1, keepdims=True))
    hid_ref[:, width:] = jnp.broadcast_to(gate, (hidden.shape[0], LANES))
    if sent is not None:
        sent.start()
    take = spot((buf_ref.shape[0], normed.shape[0]), 0) == line_ref[...]
    buf_ref[...] = dot(jnp.where(take, 1.0, 0.0).astype(BF), normed).astype(BF)


def post_first_body(shard_rows, orders, me_ref, *refs):
    pieces, (ctx_ref, res_ref, *small) = refs[:8], refs[8:14]
    hid_ref, buf_ref, w_ref, w_s, hid_s, sem = refs[14:]
    place_rows(shard_rows, orders, me_ref[0], pieces, w_s)
    kept = pltpu.make_async_copy(w_s, w_ref, sem.at[0])
    kept.start()
    sent = pltpu.make_async_copy(hid_s, hid_ref, sem.at[1])
    post_rows(ctx_ref[...], res_ref[...], w_s[...], *small, hid_s, buf_ref, sent)
    kept.wait()
    sent.wait()


def post_later_body(w_ref, ctx_ref, res_ref, *refs):
    post_rows(ctx_ref[...], res_ref[...], w_ref[...], *refs)


def moved(undo, values):
    total = None
    for _ in range(3):
        part = values.astype(BF)
        values = values - part.astype(F32)
        term = dot(undo, part)
        total = term if total is None else total + term
    return total


def settle_body(ret_ref, left_ref, *refs):
    sides, (total_ref, need_ref) = (refs[:5], refs[5:10]), refs[10:]
    width = total_ref.shape[1]
    for index, (hid, undo, slot, chosen, rank) in enumerate(sides):
        rows = undo.shape[1]
        own = chosen[...] == spot((rows, left_ref.shape[1]), 1)
        left = jnp.sum(jnp.where(own, left_ref[...], 0.0), axis=1, keepdims=True)
        factor = jnp.where(rank[...].astype(F32) < left, hid[:, width:], 0.0)
        back = moved(undo[...], hid[:, :width])
        if index == 0:
            take = jnp.where(spot((rows, ret_ref.shape[0]), 1) == slot[...], 1.0, 0.0).astype(BF)
            pick = dot(undo[...], take).astype(BF)
            factor = moved(undo[...], factor)
            total_ref[...] = back + factor[:, :1] * dot(pick, ret_ref[...])
        else:
            total_ref[...] = total_ref[...] + back
            later = jnp.where(spot(factor.shape, 1) == 0, factor, (slot[...] + 1).astype(F32))
            need_ref[...] = moved(undo[...], later)


def finish_body(ret_ref, total_ref, need_ref, out_ref, out_s, sem):
    factor = need_ref[:, :1]
    slot = need_ref[:, 1:2].astype(I32) - 1
    width = total_ref.shape[1]
    step = width // 4
    pick = spot((total_ref.shape[0], ret_ref.shape[0]), 1) == slot
    pick = jnp.where(pick, 1.0, 0.0).astype(BF)
    sent = []
    for index in range(4):
        here = slice(index * step, (index + 1) * step)
        picked = factor * dot(pick, ret_ref[:, here])
        out_s[:, here] = (total_ref[:, here] + picked).astype(BF)
        sent.append(
            pltpu.make_async_copy(
                out_s.at[:, pl.ds(index * step, step)],
                out_ref.at[:, pl.ds(index * step, step)],
                sem.at[index],
            )
        )
        sent[-1].start()
    for copy in sent:
        copy.wait()


def shards(
    tokens,
    expert_ids,
    w_qkv,
    w_attn_out,
    gain_attn,
    gain_expert,
    router,
    expert_in,
    expert_out,
    capacity,
    swap_list,
):
    seq_len, width = tokens.shape
    shard_rows = w_qkv.shape[0]
    experts_all = router.shape[1]
    dev_count = lax.axis_size("dev")
    me = lax.axis_index(AXES)
    orders = stage_orders()
    order_o = orders[0]
    parts = dealt(seq_len)
    bound = max(2, 2 * seq_len // experts_all)
    slots = (-(-bound // DEAL), bound - bound // DEAL)
    sds = jax.ShapeDtypeStruct

    pieces_q = gather(w_qkv[:, :width], orders[0])
    pieces_k = gather(w_qkv[:, width : 2 * width], orders[1])
    pieces_v = gather(w_qkv[:, 2 * width :], orders[2])

    shapes = [sds((seq_len, seq_len), BF)]
    for rows in parts:
        shapes += [sds((seq_len, rows), BF)] + [sds((rows, 1), I32)] * 3 + [sds((1, rows), I32)]
    order, *made = call(
        functools.partial(index_body, slots, experts_all),
        tuple(shapes),
        expert_ids.reshape(1, seq_len),
        flops=4 * seq_len * seq_len * experts_all,
    )
    undo, chosen, rank, slot, line = ([made[k], made[k + 5]] for k in range(5))

    tail = -(-experts_all // LANES) * LANES
    named = expert_ids == jnp.arange(tail, dtype=I32)[None, :]
    counts = jnp.sum(named.astype(F32), axis=0, keepdims=True).astype(BF)
    count_block = jnp.pad(counts, ((0, shard_rows - 1), (0, 0)))
    out_shard = jnp.concatenate([w_attn_out, count_block], axis=1)
    cut = width // 2
    shared = min(2, len(order_o) - 1)
    pieces_o = gather_cut(out_shard, orders[:2], shared, cut)

    me_word = me.reshape(1).astype(I32)
    vm = pl.BlockSpec(memory_space=pltpu.VMEM)
    sm = pl.BlockSpec(memory_space=pltpu.SMEM)
    hbm = pl.BlockSpec(memory_space=pl.ANY)
    made = call(
        functools.partial(mix_body, order_o, shard_rows),
        (
            sds((parts[0], width), BF),
            sds((parts[1], width), BF),
            sds((parts[0], width), BF),
            sds((parts[1], width), BF),
        ),
        me_word,
        order,
        tokens,
        gain_attn,
        in_specs=[sm, vm, vm, vm],
        flops=2 * seq_len * width * width,
    )
    residual, x = list(made[:2]), list(made[2:])

    head_size = width // HEADS
    group = min(width, max(256, head_size))
    pieces = len(pieces_q)
    stretches = [runs(o, order_o) for o in orders]

    def whole(*shape):
        return pl.BlockSpec(shape, lambda g: (0, 0))

    def striped(height):
        return pl.BlockSpec((height, group), lambda g: (0, g))

    stripes = [striped(width // pieces)] * pieces
    tall = striped(seq_len)
    context, keys, values = call(
        functools.partial(project_body, head_size, shard_rows, stretches),
        (
            pltpu.VMEM((parts[0], width), BF),
            pltpu.HBM((seq_len, width), BF),
            pltpu.HBM((seq_len, width), BF),
        ),
        *[far(value) for value in x + pieces_q + pieces_k + pieces_v],
        grant=GRANT,
        flops=5 * seq_len * width * width + 16 * parts[0] * seq_len * width,
        grid=(width // group,),
        in_specs=[whole(parts[0], width), whole(parts[1], width)] + stripes * 3,
        out_specs=[striped(parts[0]), tall, tall],
    )
    context_later = call(
        functools.partial(attend_body, head_size, shard_rows, stretches[0]),
        sds((parts[1], width), BF),
        x[1],
        keys,
        values,
        *pieces_q,
        flops=16 * parts[1] * seq_len * width + 2 * parts[1] * width * width,
        grid=(width // group,),
        in_specs=[whole(parts[1], width), tall, tall] + stripes,
        out_specs=striped(parts[1]),
    )
    contexts = [context, context_later]

    shard_index = jnp.arange(width, dtype=I32)
    lower = (source_device(shard_index // shard_rows, orders[1], me) < me) & (
        shard_index % shard_rows == 0
    )
    counts_all = jnp.concatenate(
        [p[:, width - cut : width - cut + experts_all] for p in pieces_o[1]], axis=0
    )
    before = jnp.sum(jnp.where(lower[:, None], counts_all.astype(F32), 0.0), axis=0).astype(I32)
    expert_range = jnp.arange(experts_all, dtype=I32)
    dev_range = jnp.arange(dev_count, dtype=I32)
    flagged = jnp.any(swap_list[:, None] == dev_range[None, :], axis=0)
    dev_index = expert_range % dev_count
    role_index = expert_range // dev_count
    flag_expert = jnp.any((dev_index[:, None] == dev_range[None, :]) & flagged[None, :], axis=1)
    location = jnp.where(flag_expert, (1 - role_index) * dev_count + dev_index, expert_range)
    room = jnp.sum(
        jnp.where(location[:, None] == expert_range[None, :], capacity[None, :], 0), axis=1
    )
    left = (room - before).astype(F32).reshape(1, experts_all)

    weight_in, weight_out = expert_in[0], expert_out[0]
    hiddens, returned = [], []
    for index, rows in enumerate(parts):
        slot_count = experts_all * slots[index]
        small = (gain_expert, router.T, chosen[index], line[index])
        cost = 2 * rows * width * width + 2 * slot_count * rows * width
        if index == 0:
            hidden, buffer, w_placed = call(
                functools.partial(post_first_body, shard_rows, orders[:2]),
                (
                    pltpu.HBM((rows, width + LANES), F32),
                    pltpu.VMEM((slot_count, width), BF),
                    pltpu.HBM((width, width), BF),
                ),
                me_word,
                *[near(piece) for piece in pieces_o[0] + pieces_o[1]],
                *[near(value) for value in (contexts[0], residual[0], *small)],
                flops=cost,
                grant=GRANT,
                in_specs=[sm] + [vm] * 14,
                out_specs=[hbm, vm, hbm],
                scratch_shapes=[
                    pltpu.VMEM((width, width), BF),
                    pltpu.VMEM((rows, width + LANES), F32),
                    pltpu.SemaphoreType.DMA((2,)),
                ],
            )
        else:
            hidden, buffer = call(
                post_later_body,
                (
                    sds((rows, width + LANES), F32),
                    sds((slot_count, width), BF),
                ),
                w_placed,
                contexts[index],
                residual[index],
                *small,
                flops=cost,
            )
        hiddens.append(hidden)
        received = lax.all_to_all(buffer, AXES, split_axis=0, concat_axis=0, tiled=True)
        activ = jnp.maximum(dot(received, weight_in), 0.0).astype(BF)
        produced = dot(activ, weight_out).astype(BF)
        returned.append(
            lax.all_to_all(produced, AXES, split_axis=0, concat_axis=0, tiled=True)
        )
    sides = []
    for index in range(len(parts)):
        sides += [hiddens[index], undo[index], slot[index], chosen[index], rank[index]]
    later_slots = experts_all * slots[1]
    total, need = call(
        settle_body,
        (
            pltpu.VMEM((seq_len, width), F32),
            pltpu.VMEM((seq_len, LANES), F32),
        ),
        returned[0],
        left,
        *[far(side) for side in sides],
        flops=8 * seq_len * seq_len * width,
        grant=GRANT,
    )
    return call(
        finish_body,
        sds((seq_len, width), BF),
        near(returned[1]),
        near(total),
        near(need),
        flops=2 * seq_len * width * later_slots,
        grant=GRANT,
        out_specs=hbm,
        scratch_shapes=[pltpu.VMEM((seq_len, width), BF), pltpu.SemaphoreType.DMA((4,))],
    )


def solution(mesh):
    rows = P(AXES, None)

    return jax.shard_map(
        shards,
        mesh=mesh,
        in_specs=(
            rows,
            rows,
            rows,
            rows,
            P(),
            P(),
            P(),
            P(AXES, None, None),
            P(AXES, None, None),
            P(),
            P(),
        ),
        out_specs=rows,
        check_vma=False,
    )
```

```python
import functools
import math

import jax
import jax.numpy as jnp
from jax import lax
from jax.experimental import pallas as pl
from jax.experimental.pallas import tpu as pltpu
from jax.sharding import PartitionSpec as P


HEADS = 16
DEAL = 2
GRANT = 40 << 20
AXES = ("role", "dev")
LANES = 128
BF = jnp.bfloat16
F32 = jnp.float32
I32 = jnp.int32


def stage_orders():
    role_bits = lax.axis_size("role").bit_length() - 1
    dev_bits = lax.axis_size("dev").bit_length() - 1
    tops = list(range(dev_bits, dev_bits + role_bits))
    mids = list(range(dev_bits - 1, 0, -1))
    near, rest = mids[:2], mids[2:]
    return near + tops + rest, near + rest + tops, tops + rest + near


def swap(block, bit):
    count = lax.axis_size(AXES)
    return lax.ppermute(block, AXES, [(i, i ^ (1 << bit)) for i in range(count)])


def gather(shard, order):
    held = shard
    for bit in order[:-1]:
        held = jnp.concatenate([held, swap(held, bit)], axis=0)
    last = swap(held, order[-1])
    return [held, last, swap(held, 0), swap(last, 0)]


def gather_cut(shard, orders, shared, cut):
    held = shard
    for stage in range(shared):
        held = jnp.concatenate([held, swap(held, orders[0][stage])], axis=0)
    sides = []
    for part, order in zip((held[:, :cut], held[:, cut:]), orders):
        for bit in order[shared:-1]:
            moved = swap(part, bit)
            part = jnp.concatenate([part, moved], axis=0)
        sides.append([part, swap(part, order[-1])])
    return [[part, last, swap(part, 0), swap(last, 0)] for part, last in sides]


def source_device(slot, order, me):
    offset = jnp.zeros_like(slot)
    for place, bit in enumerate(list(order) + [0]):
        offset = offset + (((slot >> place) & 1) << bit)
    return offset ^ me


def offsets(order):
    made = [0]
    for bit in list(order) + [0]:
        made = made + [offset ^ (1 << bit) for offset in made]
    return made


def runs(order, target):
    held = offsets(order)
    places = [held.index(offset) for offset in offsets(target)]
    per = len(places) // 4
    stretches = []
    for start in range(0, len(places), per):
        made = []
        for place in places[start : start + per]:
            piece, first = place // per, place % per
            if made and made[-1][0] == piece and made[-1][1] + made[-1][2] == first:
                made[-1][2] += 1
            else:
                made.append([piece, first, 1])
        stretches.append(made)
    return stretches


def column_order(order, me, width, shard_rows):
    wanted = lax.broadcasted_iota(I32, (1, width), 1)
    source = source_device(wanted // shard_rows, order, me) * shard_rows + wanted % shard_rows
    rows = lax.broadcasted_iota(I32, (width, width), 0)
    return jnp.where(rows == source, 1.0, 0.0).astype(BF)


def dot(left, right):
    return jnp.dot(left, right, preferred_element_type=F32)


def rms_scale(values, gain):
    mean_sq = jnp.mean(values * values, axis=-1, keepdims=True)
    return values * lax.rsqrt(mean_sq + 1e-06) * gain.astype(F32)


def far(value):
    return pltpu.with_memory_space_constraint(value, pltpu.HBM)


def near(value):
    return pltpu.with_memory_space_constraint(value, pltpu.VMEM)


def call(body, out_shape, *operands, flops=0, in_specs=None, grant=None, **kw):
    leaves = list(operands) + jax.tree.leaves(out_shape)
    moved = sum(math.prod(leaf.shape) * leaf.dtype.itemsize for leaf in leaves)
    return pl.pallas_call(
        body,
        out_shape=out_shape,
        compiler_params=pltpu.CompilerParams(vmem_limit_bytes=grant),
        in_specs=in_specs or [pl.BlockSpec(memory_space=pltpu.VMEM)] * len(operands),
        cost_estimate=pl.CostEstimate(
            flops=int(flops), bytes_accessed=int(moved), transcendentals=0
        ),
        **kw,
    )(*operands)


def spot(shape, axis):
    return lax.broadcasted_iota(I32, shape, axis)


def dealt(rows):
    return rows // DEAL, rows - rows // DEAL


def index_body(slots, experts, row_ref, *outs):
    n = row_ref.shape[1]
    first_rows = dealt(n)[0]
    down, across = spot((n, n), 0), spot((n, n), 1)
    ids_r = row_ref[...].astype(F32)
    ids_c = jnp.sum(jnp.where(down == across, ids_r, 0.0), axis=1, keepdims=True)
    match = jnp.where(ids_c.astype(I32) == spot((n, experts), 1), 1.0, 0.0)
    match_t = jnp.where(row_ref[...] == spot((experts, n), 0), 1.0, 0.0)
    rank_c = jnp.sum(
        match * dot(jnp.where(across < down, 1.0, 0.0).astype(BF), match.astype(BF)),
        axis=1,
        keepdims=True,
    )
    rank_r = jnp.sum(
        match_t * dot(match_t.astype(BF), jnp.where(down < across, 1.0, 0.0).astype(BF)),
        axis=0,
        keepdims=True,
    )
    count_r = jnp.sum(match, axis=0, keepdims=True)
    count_c = jnp.sum(match_t, axis=1, keepdims=True)
    e_down, e_across = spot((experts, experts), 0), spot((experts, experts), 1)
    first_r = jnp.sum(jnp.where(e_down < e_across, count_c, 0.0), axis=0, keepdims=True)
    first_c = jnp.sum(jnp.where(e_across < e_down, count_r, 0.0), axis=1, keepdims=True)
    start_c = jnp.sum(match * first_r, axis=1, keepdims=True)
    start_r = jnp.sum(match_t * first_c, axis=0, keepdims=True)

    def places(ids, start, rank):
        ids, start, rank = ids.astype(I32), start.astype(I32), rank.astype(I32)
        at = start + rank
        turn, left = lax.div(at, DEAL), lax.rem(at, DEAL)
        early = left == 0
        place = jnp.where(early, turn, first_rows + turn * (DEAL - 1) + left - 1)
        ahead = lax.div(at + (DEAL - 1), DEAL) - lax.div(start + (DEAL - 1), DEAL)
        slot = jnp.where(early, ids * slots[0] + ahead, ids * slots[1] + rank - ahead)
        return place, slot.astype(F32)

    place_c, slot_c = places(ids_c, start_c, rank_c)
    place_r, slot_r = places(ids_r, start_r, rank_r)
    order = place_r == down
    undo = place_c == across
    order_ref, outs = outs[0], outs[1:]
    order_ref[...] = jnp.where(order, 1.0, 0.0).astype(BF)
    undone = jnp.where(undo, 1.0, 0.0).astype(BF)

    def column(line):
        return jnp.sum(jnp.where(order, line, 0.0), axis=1, keepdims=True).astype(I32)

    columns = [column(ids_r), column(rank_r), column(slot_r)]
    line = jnp.sum(jnp.where(undo, slot_c, 0.0), axis=0, keepdims=True).astype(I32)
    for index, (low, high) in enumerate(((0, first_rows), (first_rows, n))):
        undo_ref, chosen_ref, rank_ref, slot_ref, line_ref = outs[index * 5 : index * 5 + 5]
        undo_ref[...] = undone[:, low:high]
        for ref, made in zip((chosen_ref, rank_ref, slot_ref), columns):
            ref[...] = made[low:high]
        line_ref[...] = line[:, low:high]


def mix_body(order, shard_rows, me_ref, order_ref, tok_ref, gain_ref, res0_ref, res1_ref, x_ref, x1_ref):
    width = tok_ref.shape[1]
    moved = dot(order_ref[...], tok_ref[...])
    first_rows = res0_ref.shape[0]
    res0_ref[...] = moved[:first_rows].astype(BF)
    res1_ref[...] = moved[first_rows:].astype(BF)
    normed = rms_scale(moved, gain_ref[...].reshape(1, width)).astype(BF)
    mixer = column_order(order, me_ref[0], width, shard_rows)
    mixed = dot(normed, mixer).astype(BF)
    x_ref[...] = mixed
    x1_ref[...] = mixed[first_rows:]


def attend(queries, keys, values, head_size, ahead=False):
    scale = head_size ** (-0.5)
    pair = max(1, LANES // head_size)
    wide = pair * head_size
    rows, total = queries.shape
    lane = spot((rows, wide), 1) // head_size
    ones = jnp.ones((keys.shape[0], wide), BF)

    def score(start):
        q = queries[:, start : start + wide]
        stacked = jnp.concatenate(
            [jnp.where(lane == head, q, jnp.zeros_like(q)) for head in range(pair)], axis=0
        )
        return lax.dot_general(
            stacked,
            keys[:, start : start + wide],
            (((1,), (1,)), ((), ())),
            preferred_element_type=F32,
        )

    def mix(start, scores):
        v = jnp.concatenate([values[:, start : start + wide], ones], axis=1)
        top = jnp.max(scores, axis=1, keepdims=True)
        both = dot(jnp.exp((scores - top) * scale).astype(BF), v)
        ratio = both[:, :wide] / both[:, wide:]
        out = ratio[:rows]
        for head in range(1, pair):
            out = jnp.where(lane == head, ratio[head * rows : (head + 1) * rows], out)
        return out.astype(BF)

    starts = range(0, total, wide)
    if ahead:
        made = [score(start) for start in starts]
        outs = [mix(start, scores) for start, scores in zip(starts, made)]
    else:
        outs = [mix(start, score(start)) for start in starts]
    return jnp.concatenate(outs, axis=1)


def times(x, pieces, stretches, shard_rows):
    total = None
    for index, stretch in enumerate(stretches):
        depth = shard_rows * sum(shards for _, _, shards in stretch)
        taken = [
            pieces[piece][first * shard_rows : (first + shards) * shard_rows, :]
            for piece, first, shards in stretch
        ]
        w = taken[0] if len(taken) == 1 else jnp.concatenate(taken, axis=0)
        term = dot(x[:, index * depth : (index + 1) * depth], w)
        total = term if total is None else total + term
    return total


def project_body(head_size, shard_rows, stretches, x_ref, *refs):
    ws, (ctx_ref, k_ref, v_ref) = refs[:-3], refs[-3:]
    count = len(ws) // 3
    x = x_ref[...]
    x0 = x[: ctx_ref.shape[0]]
    q = times(x0, ws[:count], stretches[0], shard_rows).astype(BF)
    k = times(x, ws[count : 2 * count], stretches[1], shard_rows).astype(BF)
    v = times(x, ws[2 * count :], stretches[2], shard_rows).astype(BF)
    k_ref[...] = k
    v_ref[...] = v
    ctx_ref[...] = attend(q, k, v, head_size)


def attend_body(head_size, shard_rows, stretches, x_ref, k_ref, v_ref, *refs):
    ws, ctx_ref = refs[:-1], refs[-1]
    q = times(x_ref[...], ws, stretches, shard_rows).astype(BF)
    ctx_ref[...] = attend(q, k_ref[...], v_ref[...], head_size, ahead=True)


def place_rows(shard_rows, orders, me, pieces, whole_ref):
    half = whole_ref.shape[1] // 2
    for side, order in enumerate(orders):
        held = offsets(order)
        per = len(held) // 4
        for place, offset in enumerate(held):
            at = pl.multiple_of((me ^ offset) * shard_rows, shard_rows)
            first = (place % per) * shard_rows
            whole_ref[pl.ds(at, shard_rows), side * half : (side + 1) * half] = pieces[
                side * 4 + place // per
            ][first : first + shard_rows, :half]


def post_rows(ctx, res, w, gain_ref, router_ref, chosen_ref, line_ref, hid_ref, buf_ref, sent=None):
    width = ctx.shape[1]
    hidden = res.astype(F32) + dot(ctx, w)
    hid_ref[:, :width] = hidden
    normed = rms_scale(hidden, gain_ref[...].reshape(1, width)).astype(BF)
    logits = lax.dot_general(
        normed, router_ref[...], (((1,), (1,)), ((), ())), preferred_element_type=F32
    )
    own = chosen_ref[...] == spot(logits.shape, 1)
    gate = jax.nn.sigmoid(jnp.sum(jnp.where(own, logits, 0.0), axis=1, keepdims=True))
    hid_ref[:, width:] = jnp.broadcast_to(gate, (hidden.shape[0], LANES))
    if sent is not None:
        sent.start()
    take = spot((buf_ref.shape[0], normed.shape[0]), 0) == line_ref[...]
    buf_ref[...] = dot(jnp.where(take, 1.0, 0.0).astype(BF), normed).astype(BF)


def post_first_body(shard_rows, orders, me_ref, *refs):
    pieces, (ctx_ref, res_ref, *small) = refs[:8], refs[8:14]
    hid_ref, buf_ref, w_ref, w_s, hid_s, sem = refs[14:]
    place_rows(shard_rows, orders, me_ref[0], pieces, w_s)
    kept = pltpu.make_async_copy(w_s, w_ref, sem.at[0])
    kept.start()
    sent = pltpu.make_async_copy(hid_s, hid_ref, sem.at[1])
    post_rows(ctx_ref[...], res_ref[...], w_s[...], *small, hid_s, buf_ref, sent)
    kept.wait()
    sent.wait()


def post_later_body(w_ref, ctx_ref, res_ref, *refs):
    post_rows(ctx_ref[...], res_ref[...], w_ref[...], *refs)


def moved(undo, values):
    total = None
    for _ in range(3):
        part = values.astype(BF)
        values = values - part.astype(F32)
        term = dot(undo, part)
        total = term if total is None else total + term
    return total


def settle_body(ret_ref, left_ref, *refs):
    sides, (total_ref, need_ref) = (refs[:5], refs[5:10]), refs[10:]
    width = total_ref.shape[1]
    for index, (hid, undo, slot, chosen, rank) in enumerate(sides):
        rows = undo.shape[1]
        own = chosen[...] == spot((rows, left_ref.shape[1]), 1)
        left = jnp.sum(jnp.where(own, left_ref[...], 0.0), axis=1, keepdims=True)
        factor = jnp.where(rank[...].astype(F32) < left, hid[:, width:], 0.0)
        back = moved(undo[...], hid[:, :width])
        if index == 0:
            take = jnp.where(spot((rows, ret_ref.shape[0]), 1) == slot[...], 1.0, 0.0).astype(BF)
            pick = dot(undo[...], take).astype(BF)
            factor = moved(undo[...], factor)
            total_ref[...] = back + factor[:, :1] * dot(pick, ret_ref[...])
        else:
            total_ref[...] = total_ref[...] + back
            later = jnp.where(spot(factor.shape, 1) == 0, factor, (slot[...] + 1).astype(F32))
            need_ref[...] = moved(undo[...], later)


def finish_body(ret_ref, total_ref, need_ref, out_ref, out_s, sem):
    factor = need_ref[:, :1]
    slot = need_ref[:, 1:2].astype(I32) - 1
    width = total_ref.shape[1]
    step = width // 4
    pick = spot((total_ref.shape[0], ret_ref.shape[0]), 1) == slot
    pick = jnp.where(pick, 1.0, 0.0).astype(BF)
    sent = []
    for index in range(4):
        here = slice(index * step, (index + 1) * step)
        picked = factor * dot(pick, ret_ref[:, here])
        out_s[:, here] = (total_ref[:, here] + picked).astype(BF)
        sent.append(
            pltpu.make_async_copy(
                out_s.at[:, pl.ds(index * step, step)],
                out_ref.at[:, pl.ds(index * step, step)],
                sem.at[index],
            )
        )
        sent[-1].start()
    for copy in sent:
        copy.wait()


def shards(
    tokens,
    expert_ids,
    w_qkv,
    w_attn_out,
    gain_attn,
    gain_expert,
    router,
    expert_in,
    expert_out,
    capacity,
    swap_list,
):
    seq_len, width = tokens.shape
    shard_rows = w_qkv.shape[0]
    experts_all = router.shape[1]
    dev_count = lax.axis_size("dev")
    me = lax.axis_index(AXES)
    orders = stage_orders()
    order_o = orders[0]
    parts = dealt(seq_len)
    bound = max(2, 2 * seq_len // experts_all)
    slots = (-(-bound // DEAL), bound - bound // DEAL)
    sds = jax.ShapeDtypeStruct

    pieces_q = gather(w_qkv[:, :width], orders[0])
    pieces_k = gather(w_qkv[:, width : 2 * width], orders[1])
    pieces_v = gather(w_qkv[:, 2 * width :], orders[2])

    shapes = [sds((seq_len, seq_len), BF)]
    for rows in parts:
        shapes += [sds((seq_len, rows), BF)] + [sds((rows, 1), I32)] * 3 + [sds((1, rows), I32)]
    order, *made = call(
        functools.partial(index_body, slots, experts_all),
        tuple(shapes),
        expert_ids.reshape(1, seq_len),
        flops=4 * seq_len * seq_len * experts_all,
    )
    undo, chosen, rank, slot, line = ([made[k], made[k + 5]] for k in range(5))

    tail = -(-experts_all // LANES) * LANES
    named = expert_ids == jnp.arange(tail, dtype=I32)[None, :]
    counts = jnp.sum(named.astype(F32), axis=0, keepdims=True).astype(BF)
    count_block = jnp.pad(counts, ((0, shard_rows - 1), (0, 0)))
    out_shard = jnp.concatenate([w_attn_out, count_block], axis=1)
    cut = width // 2
    shared = min(2, len(order_o) - 1)
    pieces_o = gather_cut(out_shard, orders[:2], shared, cut)

    me_word = me.reshape(1).astype(I32)
    vm = pl.BlockSpec(memory_space=pltpu.VMEM)
    sm = pl.BlockSpec(memory_space=pltpu.SMEM)
    hbm = pl.BlockSpec(memory_space=pl.ANY)
    made = call(
        functools.partial(mix_body, order_o, shard_rows),
        (
            sds((parts[0], width), BF),
            sds((parts[1], width), BF),
            pltpu.VMEM((seq_len, width), BF),
            sds((parts[1], width), BF),
        ),
        me_word,
        order,
        tokens,
        gain_attn,
        in_specs=[sm, vm, vm, vm],
        flops=2 * seq_len * width * width,
    )
    residual, x = list(made[:2]), list(made[2:])

    head_size = width // HEADS
    group = min(width, max(1024, head_size))
    pieces = len(pieces_q)
    stretches = [runs(o, order_o) for o in orders]

    def whole(*shape):
        return pl.BlockSpec(shape, lambda g: (0, 0))

    def striped(height):
        return pl.BlockSpec((height, group), lambda g: (0, g))

    stripes = [striped(width // pieces)] * pieces
    tall = striped(seq_len)
    context, keys, values = call(
        functools.partial(project_body, head_size, shard_rows, stretches),
        (
            pltpu.VMEM((parts[0], width), BF),
            pltpu.HBM((seq_len, width), BF),
            pltpu.HBM((seq_len, width), BF),
        ),
        near(x[0]),
        *[far(value) for value in pieces_q + pieces_k[:3]],
        near(pieces_k[3]),
        *[far(value) for value in pieces_v[:3]],
        near(pieces_v[3]),
        grant=GRANT,
        flops=5 * seq_len * width * width + 16 * parts[0] * seq_len * width,
        grid=(width // group,),
        in_specs=[whole(seq_len, width)] + stripes * 3,
        out_specs=[striped(parts[0]), tall, tall],
    )
    context_later = call(
        functools.partial(attend_body, head_size, shard_rows, stretches[0]),
        sds((parts[1], width), BF),
        x[1],
        keys,
        values,
        *pieces_q,
        flops=16 * parts[1] * seq_len * width + 2 * parts[1] * width * width,
        grid=(width // group,),
        in_specs=[whole(parts[1], width), tall, tall] + stripes,
        out_specs=striped(parts[1]),
    )
    contexts = [context, context_later]

    shard_index = jnp.arange(width, dtype=I32)
    lower = (source_device(shard_index // shard_rows, orders[1], me) < me) & (
        shard_index % shard_rows == 0
    )
    counts_all = jnp.concatenate(
        [p[:, width - cut : width - cut + experts_all] for p in pieces_o[1]], axis=0
    )
    before = jnp.sum(jnp.where(lower[:, None], counts_all.astype(F32), 0.0), axis=0).astype(I32)
    expert_range = jnp.arange(experts_all, dtype=I32)
    dev_range = jnp.arange(dev_count, dtype=I32)
    flagged = jnp.any(swap_list[:, None] == dev_range[None, :], axis=0)
    dev_index = expert_range % dev_count
    role_index = expert_range // dev_count
    flag_expert = jnp.any((dev_index[:, None] == dev_range[None, :]) & flagged[None, :], axis=1)
    location = jnp.where(flag_expert, (1 - role_index) * dev_count + dev_index, expert_range)
    room = jnp.sum(
        jnp.where(location[:, None] == expert_range[None, :], capacity[None, :], 0), axis=1
    )
    left = (room - before).astype(F32).reshape(1, experts_all)

    weight_in, weight_out = expert_in[0], expert_out[0]
    hiddens, returned = [], []
    for index, rows in enumerate(parts):
        slot_count = experts_all * slots[index]
        small = (gain_expert, router.T, chosen[index], line[index])
        cost = 2 * rows * width * width + 2 * slot_count * rows * width
        if index == 0:
            hidden, buffer, w_placed = call(
                functools.partial(post_first_body, shard_rows, orders[:2]),
                (
                    pltpu.HBM((rows, width + LANES), F32),
                    pltpu.VMEM((slot_count, width), BF),
                    pltpu.HBM((width, width), BF),
                ),
                me_word,
                *[near(piece) for piece in pieces_o[0] + pieces_o[1]],
                *[near(value) for value in (contexts[0], residual[0], *small)],
                flops=cost,
                grant=GRANT,
                in_specs=[sm] + [vm] * 14,
                out_specs=[hbm, vm, hbm],
                scratch_shapes=[
                    pltpu.VMEM((width, width), BF),
                    pltpu.VMEM((rows, width + LANES), F32),
                    pltpu.SemaphoreType.DMA((2,)),
                ],
            )
        else:
            hidden, buffer = call(
                post_later_body,
                (
                    sds((rows, width + LANES), F32),
                    sds((slot_count, width), BF),
                ),
                w_placed,
                contexts[index],
                residual[index],
                *small,
                flops=cost,
            )
        hiddens.append(hidden)
        received = lax.all_to_all(buffer, AXES, split_axis=0, concat_axis=0, tiled=True)
        activ = jnp.maximum(dot(received, weight_in), 0.0).astype(BF)
        produced = dot(activ, weight_out).astype(BF)
        returned.append(
            lax.all_to_all(produced, AXES, split_axis=0, concat_axis=0, tiled=True)
        )
    sides = []
    for index in range(len(parts)):
        sides += [hiddens[index], undo[index], slot[index], chosen[index], rank[index]]
    later_slots = experts_all * slots[1]
    total, need = call(
        settle_body,
        (
            pltpu.VMEM((seq_len, width), F32),
            pltpu.VMEM((seq_len, LANES), F32),
        ),
        returned[0],
        left,
        *[far(side) for side in sides],
        flops=8 * seq_len * seq_len * width,
        grant=GRANT,
    )
    return call(
        finish_body,
        sds((seq_len, width), BF),
        near(returned[1]),
        near(total),
        near(need),
        flops=2 * seq_len * width * later_slots,
        grant=GRANT,
        out_specs=hbm,
        scratch_shapes=[pltpu.VMEM((seq_len, width), BF), pltpu.SemaphoreType.DMA((4,))],
    )


def solution(mesh):
    rows = P(AXES, None)

    return jax.shard_map(
        shards,
        mesh=mesh,
        in_specs=(
            rows,
            rows,
            rows,
            rows,
            P(),
            P(),
            P(),
            P(AXES, None, None),
            P(AXES, None, None),
            P(),
            P(),
        ),
        out_specs=rows,
        check_vma=False,
    )
```
